32 devices in a mesh: grp: 1, seq: 16 (over z, y, x), head: 1, srv: 2 (over core).
Axes of the slice: x: 2, y: 2, z: 4, core: 2. Of those that a mesh axis runs over, the one named last changes fastest.
Arguments:
- tokens: bfloat16 [4096, 4096], P(('grp', 'seq', 'srv'), 'head'), may hold values from -6 to 6
- norm_gain: float32 [4096], replicated, may hold values from 0.5 to 12, as said below
- wq: bfloat16 [4096, 4096], P(('seq', 'srv'), 'head'), may hold values from -0.09375 to 0.09375
- wk: bfloat16 [4096, 1024], P(('seq', 'srv'), 'head'), may hold values from -0.09375 to 0.09375
- wv: bfloat16 [4096, 1024], P(('seq', 'srv'), 'head'), may hold values from -0.09375 to 0.09375
- wo: bfloat16 [4096, 4096], P('head', ('seq', 'srv')), may hold values from -0.09375 to 0.09375
- doc_ids: int32 [4096], P(('grp', 'seq', 'srv')), may hold values from 0 to 7, never falling along the last dimension, each value on 1 to 3072 neighbouring positions
Outputs:
- mixed: bfloat16 [4096, 4096], P(('grp', 'seq', 'srv'), 'head')
The draws below stay inside these ranges and needn't reach their ends.
Inputs may be any that keep to these rules, and one draw needn't show every extreme that they name: `norm_gain`: the gain is positive.
All inputs are finite; a program needn't handle non-finite values.
Results may differ from the reference program's by a relative error of at most 0.015.
The reference program's roundings to bfloat16 on the way count: a program that leaves them out, or rounds other values in their place, can miss the bound.
Values may be sent and summed in bfloat16 or wider, within the bound.
No kernel may reach another device: no remote copies, remote signals or barrier semaphores. Data moves between devices by JAX's collectives and lax.ppermute only.
A program may use at most 128 MiB of HBM per device.

```python
import math
import jax
import jax.numpy as jnp
import numpy as np
from jax import lax

MODEL_WIDTH = 4096
QUERY_HEADS = 32
KV_HEAD_COUNT = 8
HEAD_WIDTH = 128
DOCS = 8
SEQUENCE_TOKENS = 4096
DOC_MOST = 3072
N_HEAD = 1


def draw_norm_gain(key, part):
    low_end = 0.5
    high_end = 2.0
    unit = jax.random.uniform(key, (MODEL_WIDTH,), jnp.float32)
    return jnp.exp(jnp.log(low_end) + unit * (jnp.log(high_end) - jnp.log(low_end)))


def levels(rng, dims, split, low, top_value):
    def one(position, parts):
        draws = jax.random.uniform(jax.random.fold_in(jax.random.fold_in(rng, 6), position), (parts,), jnp.float32, low / len(split), top_value / len(split))
        return jnp.repeat(jnp.exp(draws), dims[position] // parts).reshape((-1,) + (1,) * (len(dims) - position - 1))

    loudness = one(*split[0])
    for cut in split[1:]:
        loudness = loudness * one(*cut)
    return loudness


def profile(count, total, most, skew):
    portions = [(1 << 20) // math.isqrt(standing ** skew) + 1 for standing in range(2, count + 1)]
    rest, given = total - most - (count - 1), [1] * (count - 1)
    while rest > 0:
        candidates = [i for i in range(count - 1) if given[i] < most]
        pool, remaining = sum([portions[i] for i in candidates]), rest
        for i in candidates:
            addition = min(most - given[i], max(1, remaining * portions[i] // pool), rest)
            given[i] = given[i] + addition
            rest = rest - addition
    return np.array([most] + given)


def ragged(stream_key, number_of, total, bound, skew):
    if number_of == 2:
        one = jax.random.randint(stream_key, (), max(1, total - bound), min(bound, total - 1) + 1)
        return jnp.stack([one, total - one])
    tallies = jnp.asarray(profile(number_of, total, bound, skew), jnp.int32)
    couples = (number_of - 1) // 2
    donor, sink = tallies[1:1 + 2 * couples:2], tallies[2:2 + 2 * couples:2]
    slack = jnp.minimum(donor - 1, bound - sink)
    shifted = jax.random.randint(jax.random.fold_in(stream_key, 1), (couples,), 0, 1 << 20) % (slack + 1)
    tallies = tallies.at[1:1 + 2 * couples:2].set(donor - shifted).at[2:2 + 2 * couples:2].set(sink + shifted)
    return tallies[jax.random.permutation(jax.random.fold_in(stream_key, 2), number_of)]


def scatter_about(key, shape, deviation, limit, shards=(), kind=jnp.bfloat16):
    factor_of = levels(key, shape, shards, -0.22, 0.18) if shards else 1.0
    array = jax.random.normal(key, shape, jnp.float32) * deviation * factor_of
    return jnp.minimum(jnp.maximum(array, -limit), limit).astype(kind)


def setup_inputs(seed: int = 0, part: int = 0) -> dict:
    splits = jax.random.split(jax.random.key(seed), 8)
    part_splits = jax.random.split(jax.random.fold_in(splits[7], part), 8)
    return {
        "tokens": scatter_about(part_splits[0], (SEQUENCE_TOKENS, MODEL_WIDTH), 1.0, 6.0, ((0, 32),)),
        "norm_gain": draw_norm_gain(jax.random.fold_in(splits[7], 71), part),
        "wq": scatter_about(splits[2], (MODEL_WIDTH, QUERY_HEADS * HEAD_WIDTH), MODEL_WIDTH ** -0.5, 0.09375, ((0, 32),)),
        "wk": scatter_about(splits[3], (MODEL_WIDTH, KV_HEAD_COUNT * HEAD_WIDTH), MODEL_WIDTH ** -0.5, 0.09375, ((0, 32),)),
        "wv": scatter_about(splits[4], (MODEL_WIDTH, KV_HEAD_COUNT * HEAD_WIDTH), MODEL_WIDTH ** -0.5, 0.09375, ((0, 32),)),
        "wo": scatter_about(splits[5], (QUERY_HEADS * HEAD_WIDTH, MODEL_WIDTH), (QUERY_HEADS * HEAD_WIDTH) ** -0.5, 0.09375, ((1, 32),)),
        "doc_ids": jnp.searchsorted(jnp.cumsum(ragged(part_splits[6], DOCS, SEQUENCE_TOKENS, DOC_MOST, 2)), jnp.arange(SEQUENCE_TOKENS), side="right").astype(jnp.int32),
    }


def rope(field, positions):
    half = field.shape[-1] // 2
    freqs = 500000.0 ** (-(jnp.arange(half, dtype=jnp.float32) * 2.0 / field.shape[-1]))
    angles = positions.astype(jnp.float32)[:, None] * freqs[None, :]
    cosine = jnp.cos(angles)[:, None, :]
    sine = jnp.sin(angles)[:, None, :]
    first = field[..., :half]
    second = field[..., half:]
    return jnp.concatenate([first * cosine - second * sine, second * cosine + first * sine], axis=-1)

def reference(tokens, norm_gain, wq, wk, wv, wo, doc_ids):
    source = tokens.astype(jnp.float32)
    mean_sq = lax.optimization_barrier(jnp.mean(source * source, axis=1, keepdims=True))
    normed_input = (source * lax.rsqrt(mean_sq + 1e-05) * norm_gain[None, :]).astype(jnp.bfloat16)
    positions = jnp.arange(SEQUENCE_TOKENS, dtype=jnp.int32)
    query_matrix = jnp.dot(normed_input, wq, preferred_element_type=jnp.float32).reshape(SEQUENCE_TOKENS, QUERY_HEADS, HEAD_WIDTH)
    query_matrix = rope(query_matrix, positions).astype(jnp.bfloat16)
    key_matrix = jnp.dot(normed_input, wk, preferred_element_type=jnp.float32).reshape(SEQUENCE_TOKENS, KV_HEAD_COUNT, HEAD_WIDTH)
    key_matrix = rope(key_matrix, positions).astype(jnp.bfloat16)
    value_matrix = jnp.dot(normed_input, wv, preferred_element_type=jnp.float32).reshape(SEQUENCE_TOKENS, KV_HEAD_COUNT, HEAD_WIDTH).astype(jnp.bfloat16)
    query_group = QUERY_HEADS // KV_HEAD_COUNT
    token_rows = 256
    scale = 1.0 / HEAD_WIDTH ** 0.5

    def one_block(block):
        start_index = (block * token_rows).astype(jnp.int32)
        rows_of_query = lax.dynamic_slice_in_dim(query_matrix, start_index, token_rows, 0).reshape(token_rows, KV_HEAD_COUNT, query_group, HEAD_WIDTH)
        query_pos = start_index + jnp.arange(token_rows, dtype=jnp.int32)
        query_doc = lax.dynamic_slice_in_dim(doc_ids, start_index, token_rows, 0)
        allowed = (positions[None, :] <= query_pos[:, None]) & (doc_ids[None, :] == query_doc[:, None])

        def single_head(head):
            key_head = jnp.take(key_matrix, head, axis=1).astype(jnp.float32)
            value_head = jnp.take(value_matrix, head, axis=1).astype(jnp.float32)
            query_head = jnp.take(rows_of_query, head, axis=1).astype(jnp.float32)
            scores = jnp.einsum('qgd,kd->qgk', query_head, key_head) * scale
            masked = jnp.where(allowed[:, None, :], scores, -1e+30)
            top = lax.optimization_barrier(jnp.max(masked, axis=2, keepdims=True))
            expd = jnp.where(allowed[:, None, :], jnp.exp(masked - top), 0.0)
            total = lax.optimization_barrier(jnp.sum(expd, axis=2, keepdims=True))
            weights = expd.astype(jnp.bfloat16).astype(jnp.float32)
            return jnp.einsum('qgk,kd->qgd', weights, value_head) / total
        head_list = lax.map(single_head, jnp.arange(KV_HEAD_COUNT, dtype=jnp.int32))
        return jnp.transpose(head_list, (1, 0, 2, 3)).reshape(token_rows, QUERY_HEADS * HEAD_WIDTH)
    attended = lax.map(one_block, jnp.arange(SEQUENCE_TOKENS // token_rows, dtype=jnp.int32))
    attended = attended.reshape(SEQUENCE_TOKENS, QUERY_HEADS * HEAD_WIDTH).astype(jnp.bfloat16)
    width = QUERY_HEADS * HEAD_WIDTH // N_HEAD
    summed = jnp.zeros((SEQUENCE_TOKENS, MODEL_WIDTH), jnp.float32)
    for shard in range(N_HEAD):
        part_term = jnp.dot(attended[:, shard * width:(shard + 1) * width], wo[shard * width:(shard + 1) * width, :], preferred_element_type=jnp.float32)
        summed = summed + part_term.astype(jnp.bfloat16).astype(jnp.float32)
    return (source + summed).astype(jnp.bfloat16)
```

```python
import functools
import math

import jax
import jax.numpy as jnp
import numpy as np
from jax import lax
from jax.experimental import pallas as pl
from jax.experimental.pallas import tpu as pltpu
from jax.sharding import Mesh
from jax.sharding import PartitionSpec as P

QUERY_HEADS = 32
KV_HEAD_COUNT = 8
HEAD_WIDTH = 128
DOCS = 8


AXES = ("zh", "zl", "y", "x", "c")
QUAD = ("zl", "x", "c")
SWAP = [(0, 1), (1, 0)]
EXTRA = 16
QT = 256
KT = 512
NEG = -1e30

ANY = pl.BlockSpec(memory_space=pl.ANY)
VMEM = pl.BlockSpec(memory_space=pltpu.VMEM)
SMEM = pl.BlockSpec(memory_space=pltpu.SMEM)


def swap(value, axis):
    return lax.ppermute(value, axis, SWAP)


def quad_gather(block, rows):
    half = rows // 2
    by_x = swap(block, "x")
    by_z = swap(block, "zl")
    low = swap(by_x[:half], "zl")
    high = swap(by_z[half:], "x")
    got = [
        (0, 0, 0, rows, block),
        (0, 1, 0, rows, by_x),
        (1, 0, 0, rows, by_z),
        (1, 1, 0, half, low),
        (1, 1, half, half, high),
    ]
    out = []
    for dzl, dx, first, size, piece in got:
        out.append((dzl, dx, 0, first, size, piece))
        out.append((dzl, dx, 1, first, size, swap(piece, "c")))
    return out


def pair_gather(block):
    by_z = swap(block, "zh")
    return [(0, 0, block), (0, 1, swap(block, "y")), (1, 0, by_z), (1, 1, swap(by_z, "y"))]


def run_copies(copies, sems):
    started = []
    for i, (src, dst) in enumerate(copies):
        copy = pltpu.make_async_copy(src, dst, sems.at[i])
        copy.start()
        started.append(copy)
    return started


def aligned(value, step):
    return pl.multiple_of(value, step)


def project_kernel(n_tok, n_q, tok_slots, q_slots, where, *refs):
    tok_refs = refs[:n_tok]
    q_refs = refs[n_tok : n_tok + n_q]
    kv_refs = refs[n_tok + n_q : n_tok + n_q + 4]
    cos_ref, sin_ref, q_out, kv_out, xs, wq, wkv, sems = refs[n_tok + n_q + 4 :]
    zh, zl, y, x, c = (where[i] for i in range(5))
    copies = []
    for (dzl, dx, dc, first, size), ref in zip(tok_slots, tok_refs):
        slot = 4 * (zl ^ dzl) + 2 * (x ^ dx) + (c ^ dc)
        row = aligned(slot * 128 + first, 64)
        copies.append((ref, xs.at[pl.ds(row, size), :]))
    for (dzh, dy, zlp), ref in zip(q_slots, q_refs):
        block = 4 * (zh ^ dzh) + 2 * zlp + (y ^ dy)
        copies.append((ref, wq.at[pl.ds(aligned(block * 512, 512), 512), :]))
    for (dzh, dy), ref in zip(((0, 0), (0, 1), (1, 0), (1, 1)), kv_refs):
        for j in range(8):
            block = 4 * (zh ^ dzh) + 2 * (j // 4) + (y ^ dy)
            row = aligned(block * 512 + (j % 4) * 128, 128)
            copies.append((ref.at[j, pl.ds(0, 128), :], wkv.at[pl.ds(row, 128), :]))
    for copy in run_copies(copies, sems):
        copy.wait()

    def turn(part, rows):
        return part * cos_ref[rows, :] + pltpu.roll(part, 64, axis=1) * sin_ref[rows, :]

    @pl.loop(0, 2)
    def _(m):
        rows = pl.ds(aligned(m * 512, 512), 512)
        left = xs[rows, :]
        acc = jnp.dot(left, wkv[...], preferred_element_type=jnp.float32)
        kv_out[rows, :128] = turn(acc[:, :128], rows).astype(jnp.bfloat16)
        kv_out[rows, 128:] = acc[:, 128:].astype(jnp.bfloat16)
        for n in range(2):
            acc = jnp.dot(left, wq[:, 256 * n : 256 * n + 256], preferred_element_type=jnp.float32)
            q_out[rows, 256 * n : 256 * n + 128] = turn(acc[:, :128], rows).astype(jnp.bfloat16)
            q_out[rows, 256 * n + 128 : 256 * n + 256] = turn(acc[:, 128:], rows).astype(jnp.bfloat16)


def attend_kernel(where, tile_lo, tile_hi, q_ref, start_ref, *refs):
    kv_refs = refs[:4]
    out_ref, ks, vs, top, total, acc, sems = refs[4:]
    zh, y = where[0], where[2]
    copies = []
    for (dzh, dy), ref in zip(((0, 0), (0, 1), (1, 0), (1, 1)), kv_refs):
        for zlp in range(2):
            row = aligned((4 * (zh ^ dzh) + 2 * zlp + (y ^ dy)) * 512, 512)
            for half, dst in ((0, ks), (1, vs)):
                copies.append((
                    ref.at[pl.ds(zlp * 512, 512), pl.ds(half * 128, 128)],
                    dst.at[pl.ds(row, 512), :],
                ))
    for copy in run_copies(copies, sems):
        copy.wait()
    factor = math.log2(math.e) / math.sqrt(HEAD_WIDTH)

    @pl.loop(0, 1024 // QT)
    def _(tile):
        rows = pl.ds(aligned(tile * QT, QT), QT)
        first = (2 * zh + tile * QT // 512) * 1024 + y * 512 + (tile * QT) % 512
        low, high = tile_lo[tile], tile_hi[tile]
        queries = jnp.concatenate([q_ref[rows, 128 * h : 128 * h + 128] for h in range(4)], axis=0)
        top[...] = jnp.full_like(top, NEG)
        total[...] = jnp.zeros_like(total)
        acc[...] = jnp.zeros_like(acc)

        def step(block, masked):
            keys = pl.ds(aligned(block * KT, KT), KT)
            scores = lax.dot_general(
                queries, ks[keys, :], (((1,), (1,)), ((), ())), preferred_element_type=jnp.float32
            )
            if masked:
                key_pos = block * KT + lax.broadcasted_iota(jnp.int32, (QT, KT), 1)
                query_pos = first + lax.broadcasted_iota(jnp.int32, (QT, KT), 0)
                seen = (key_pos <= query_pos) & (key_pos >= start_ref[rows, :1])
                scores = jnp.where(seen[None], scores.reshape(4, QT, KT), NEG).reshape(4 * QT, KT)
            best = scores[:, :128]
            for i in range(1, KT // 128):
                best = jnp.maximum(best, scores[:, 128 * i : 128 * i + 128])
            old = top[...]
            new = jnp.maximum(old, jnp.max(best, axis=1, keepdims=True))
            top[...] = new
            shrink = jnp.exp2((old - new) * factor)
            parts = [
                jnp.exp2((scores[:, 128 * i : 128 * i + 128] - new) * factor)
                for i in range(KT // 128)
            ]
            total[...] = total[...] * shrink + functools.reduce(jnp.add, parts)
            weights = jnp.concatenate([part.astype(jnp.bfloat16) for part in parts], axis=1)
            acc[...] = acc[...] * shrink + jnp.dot(
                weights, vs[keys, :], preferred_element_type=jnp.float32
            )

        @pl.loop(low // KT, (first + QT + KT - 1) // KT)
        def _(block):
            edge = (block * KT + KT - 1 > first) | (block * KT < high)

            @pl.when(edge)
            def _():
                step(block, True)

            @pl.when(jnp.logical_not(edge))
            def _():
                step(block, False)

        result = acc[...] / jnp.sum(total[...], axis=1, keepdims=True)
        for h in range(4):
            out_ref[rows, 128 * h : 128 * h + 128] = result[QT * h : QT * h + QT].astype(jnp.bfloat16)


def output_kernel(n_att, att_slots, where, *refs):
    att_refs = refs[:n_att]
    wo_refs = refs[n_att : n_att + 4]
    out_ref, xs, wo, sems = refs[n_att + 4 :]
    zh, zl, y, x, c = (where[i] for i in range(5))
    copies = []
    for (dzl, dx, dc, first, size), ref in zip(att_slots, att_refs):
        slot = 4 * (zl ^ dzl) + 2 * (x ^ dx) + (c ^ dc)
        copies.append((ref, xs.at[pl.ds(first, size), pl.ds(aligned(slot * 512, 512), 512)]))
    for (dzh, dy), ref in zip(((0, 0), (0, 1), (1, 0), (1, 1)), wo_refs):
        column = aligned((2 * (zh ^ dzh) + (y ^ dy)) * 128, 128)
        copies.append((ref, wo.at[:, pl.ds(column, 128)]))
    for copy in run_copies(copies, sems):
        copy.wait()

    @pl.loop(0, 2)
    def _(m):
        rows = pl.ds(aligned(m * 512, 512), 512)
        left = xs[rows, :]
        for n in range(2):
            acc = jnp.dot(left, wo[:, 256 * n : 256 * n + 256], preferred_element_type=jnp.float32)
            out_ref[rows, 256 * n : 256 * n + 256] = acc.astype(jnp.bfloat16)


def finish_kernel(tok_ref, sent_ref, out_ref):
    for block in range(32):
        zhp, zlp, yp, xp, cp = ((block >> s) & 1 for s in (4, 3, 2, 1, 0))
        source, part = 4 * zlp + 2 * xp + cp, 2 * zhp + yp
        columns = slice(128 * block, 128 * block + 128)
        sent = sent_ref[source, :, 128 * part : 128 * part + 128].astype(jnp.float32)
        out_ref[:, columns] = (tok_ref[:, columns].astype(jnp.float32) + sent).astype(jnp.bfloat16)


def call(kernel, out_shape, in_specs, scratch, cost, name):
    flops, moved = cost
    return pl.pallas_call(
        kernel,
        out_shape=out_shape,
        in_specs=in_specs,
        out_specs=jax.tree.map(lambda _: VMEM, out_shape),
        scratch_shapes=scratch,
        compiler_params=pltpu.CompilerParams(vmem_limit_bytes=48 * 1024 * 1024),
        cost_estimate=pl.CostEstimate(flops=flops, bytes_accessed=moved, transcendentals=0),
        name=name,
    )


def split_local(tokens, norm_gain, wq, wk, wv, wo, doc_ids):
    bf16, f32 = jnp.bfloat16, jnp.float32
    place = [lax.axis_index(axis) for axis in AXES]
    where = jnp.stack(place).astype(jnp.int32)
    zh, zl, y, x, c = place

    source = tokens.astype(f32)
    mean_sq = jnp.mean(source * source, axis=1, keepdims=True)
    normed = (source * lax.rsqrt(mean_sq + 1e-05) * norm_gain[None, :]).astype(bf16)

    below = jnp.sum(
        doc_ids[:, None] < lax.broadcasted_iota(jnp.int32, (1, 256), 1), axis=0, dtype=jnp.int32
    ).astype(bf16)
    wkv = jnp.concatenate([wk.reshape(128, 8, 128), wv.reshape(128, 8, 128)], axis=2)
    wkv = jnp.concatenate([wkv, jnp.broadcast_to(below, (EXTRA, 8, 256))], axis=0)
    wkv = lax.all_to_all(jnp.transpose(wkv, (1, 0, 2)), QUAD, 0, 0, tiled=True)
    wqs = jnp.transpose(wq.reshape(128, 8, 512), (1, 0, 2))
    wqs = lax.all_to_all(wqs, QUAD, 0, 0, tiled=True).reshape(2, 512, 512)

    kv_w = pair_gather(wkv)
    q_w = []
    for zlp in range(2):
        q_w += [((dzh, dy, zlp), piece) for dzh, dy, piece in pair_gather(wqs[zlp])]

    tok = quad_gather(normed, 128)

    token = jnp.arange(1024, dtype=jnp.int32)
    positions = (2 * zh + token // 512) * 1024 + y * 512 + token % 512
    freqs = 500000.0 ** (-(jnp.arange(64, dtype=f32) * 2.0 / HEAD_WIDTH))
    angles = positions.astype(f32)[:, None] * freqs[None, :]
    cosine, sine = jnp.cos(angles), jnp.sin(angles)
    cosine = jnp.concatenate([cosine, cosine], axis=1)
    sine = jnp.concatenate([-sine, sine], axis=1)

    starts = sum(jnp.sum(piece[:, 128, :DOCS].astype(f32), axis=0) for _, _, piece in kv_w)
    starts = starts.astype(jnp.int32)
    spans = (positions[:, None] >= starts[None, :])
    query_start = jnp.max(jnp.where(spans, starts[None, :], 0), axis=1)
    tile_lo = query_start[::QT]
    tile_hi = query_start[QT - 1 :: QT]
    start_col = jnp.broadcast_to(query_start[:, None], (1024, 128))

    queries, keys_values = call(
        functools.partial(
            project_kernel, len(tok), len(q_w), [t[:5] for t in tok], [s for s, _ in q_w]
        ),
        (
            jax.ShapeDtypeStruct((1024, 512), bf16),
            jax.ShapeDtypeStruct((1024, 256), bf16),
        ),
        [SMEM] + [ANY] * (len(tok) + len(q_w) + 4) + [VMEM, VMEM],
        [
            pltpu.VMEM((1024, 4096), bf16),
            pltpu.VMEM((4096, 512), bf16),
            pltpu.VMEM((4096, 256), bf16),
            pltpu.SemaphoreType.DMA((len(tok) + len(q_w) + 32,)),
        ],
        (2 * 1024 * 4096 * 768, 17 << 20),
        "project",
    )(where, *[t[5] for t in tok], *[w for _, w in q_w], *[w for _, _, w in kv_w], cosine, sine)

    by_z = lax.ppermute(keys_values, "zh", [(0, 1)])
    kv = [keys_values, swap(keys_values, "y"), by_z, swap(by_z, "y")]

    attended = call(
        attend_kernel,
        jax.ShapeDtypeStruct((1024, 512), bf16),
        [SMEM, SMEM, SMEM, VMEM, VMEM] + [ANY] * 4,
        [
            pltpu.VMEM((4096, 128), bf16),
            pltpu.VMEM((4096, 128), bf16),
            pltpu.VMEM((4 * QT, 128), f32),
            pltpu.VMEM((4 * QT, 128), f32),
            pltpu.VMEM((4 * QT, 128), f32),
            pltpu.SemaphoreType.DMA((16,)),
        ],
        (4 * 1024 * 4096 * 512, 8 << 20),
        "attend",
    )(where, tile_lo, tile_hi, queries, start_col, *kv)

    wo, unused = lax.optimization_barrier((wo, keys_values))
    wos = pair_gather(wo)

    att = quad_gather(attended, 1024)
    sent = call(
        functools.partial(output_kernel, len(att), [t[:5] for t in att]),
        jax.ShapeDtypeStruct((1024, 512), bf16),
        [SMEM] + [ANY] * (len(att) + 4),
        [
            pltpu.VMEM((1024, 4096), bf16),
            pltpu.VMEM((4096, 512), bf16),
            pltpu.SemaphoreType.DMA((len(att) + 4,)),
        ],
        (2 * 1024 * 4096 * 512, 13 << 20),
        "output",
    )(where, *[t[5] for t in att], *[w for _, _, w in wos])
    home = lax.all_to_all(sent.reshape(8, 128, 512), QUAD, 0, 0, tiled=True)
    return call(
        finish_kernel,
        jax.ShapeDtypeStruct((128, 4096), bf16),
        [VMEM, VMEM],
        [],
        (128 * 4096, 3 << 20),
        "finish",
    )(tokens, home)


def rope(field, positions):
    half = field.shape[-1] // 2
    freqs = 500000.0 ** (-(jnp.arange(half, dtype=jnp.float32) * 2.0 / field.shape[-1]))
    angles = positions.astype(jnp.float32)[:, None] * freqs[None, :]
    cosine = jnp.cos(angles)[:, None, :]
    sine = jnp.sin(angles)[:, None, :]
    first = field[..., :half]
    second = field[..., half:]
    return jnp.concatenate(
        [first * cosine - second * sine, second * cosine + first * sine], axis=-1
    )


def local(tokens, norm_gain, wq, wk, wv, wo, doc_ids):
    tok_rows = tokens.shape[0]
    head_size = HEAD_WIDTH
    kv_local = wk.shape[1] // head_size
    query_group = QUERY_HEADS // KV_HEAD_COUNT
    source = tokens.astype(jnp.float32)
    whole = lax.all_gather(tokens, "head", axis=1, tiled=True).astype(jnp.float32)
    mean_sq = jnp.mean(whole * whole, axis=1, keepdims=True)
    normed_input = (whole * lax.rsqrt(mean_sq + 1e-05) * norm_gain[None, :]).astype(jnp.bfloat16)
    query_acc = jnp.dot(
        normed_input,
        lax.all_gather(wq, ("seq", "srv"), axis=0, tiled=True),
        preferred_element_type=jnp.float32,
    )
    key_acc = jnp.dot(
        normed_input,
        lax.all_gather(wk, ("seq", "srv"), axis=0, tiled=True),
        preferred_element_type=jnp.float32,
    )
    value_acc = jnp.dot(
        normed_input,
        lax.all_gather(wv, ("seq", "srv"), axis=0, tiled=True),
        preferred_element_type=jnp.float32,
    )
    first_pos = lax.axis_index(("seq", "srv")) * tok_rows
    positions = first_pos + jnp.arange(tok_rows, dtype=jnp.int32)
    query_matrix = rope(query_acc.reshape(tok_rows, kv_local * query_group, head_size), positions)
    query_matrix = query_matrix.astype(jnp.bfloat16).reshape(
        tok_rows, kv_local, query_group, head_size
    )
    key_matrix = rope(key_acc.reshape(tok_rows, kv_local, head_size), positions).astype(
        jnp.bfloat16
    )
    key_matrix = key_matrix.reshape(tok_rows, kv_local * head_size)
    value_matrix = value_acc.astype(jnp.bfloat16)
    scale = 1.0 / head_size**0.5

    def attend_block(carry, key_rows, value_rows, doc_rows, key_pos):
        run_top, run_total, run_acc = carry
        key_heads = key_rows.reshape(key_rows.shape[0], kv_local, head_size)
        value_heads = value_rows.reshape(value_rows.shape[0], kv_local, head_size)
        scores = (
            jnp.einsum(
                "qcgd,kcd->qcgk", query_matrix, key_heads, preferred_element_type=jnp.float32
            )
            * scale
        )
        allowed = (
            (key_pos[None, :] <= positions[:, None])
            & (key_pos[None, :] >= 0)
            & (doc_rows[None, :] == doc_ids[:, None])
        )
        allowed = allowed[:, None, None, :]
        masked = jnp.where(allowed, scores, -1e30)
        new_top = jnp.maximum(run_top, jnp.max(masked, axis=3))
        expd = jnp.where(allowed, jnp.exp(masked - new_top[..., None]), 0.0)
        factor = jnp.exp(run_top - new_top)
        new_total = run_total * factor + jnp.sum(expd, axis=3)
        weights = expd.astype(jnp.bfloat16)
        update = jnp.einsum(
            "qcgk,kcd->qcgd", weights, value_heads, preferred_element_type=jnp.float32
        )
        return (new_top, new_total, run_acc * factor[..., None] + update)

    start_state = (
        jnp.full((tok_rows, kv_local, query_group), -1e30, jnp.float32),
        jnp.zeros((tok_rows, kv_local, query_group), jnp.float32),
        jnp.zeros((tok_rows, kv_local, query_group, head_size), jnp.float32),
    )
    key_piece = lax.all_gather(key_matrix, ("seq", "srv"), axis=0, tiled=True)
    value_piece = lax.all_gather(value_matrix, ("seq", "srv"), axis=0, tiled=True)
    doc_piece = lax.all_gather(doc_ids, ("seq", "srv"), axis=0, tiled=True)
    count = key_piece.shape[0]
    width = math.gcd(count, 512)

    def step(inner, index):
        offset = index * width
        key_rows = lax.dynamic_slice_in_dim(key_piece, offset, width, 0)
        value_rows = lax.dynamic_slice_in_dim(value_piece, offset, width, 0)
        doc_rows = lax.dynamic_slice_in_dim(doc_piece, offset, width, 0)
        key_pos = offset + jnp.arange(width, dtype=jnp.int32)
        return (attend_block(inner, key_rows, value_rows, doc_rows, key_pos), None)

    def run_all(inner):
        result, unused = lax.scan(step, inner, jnp.arange(count // width, dtype=jnp.int32))
        return result

    beyond = jnp.int32(0) > first_pos + tok_rows - 1
    before = doc_piece[count - 1] < doc_ids[0]
    final_top, final_total, final_acc = lax.cond(
        beyond | before, lambda inner: inner, run_all, start_state
    )
    attended = (final_acc / final_total[..., None]).astype(jnp.bfloat16)
    attended = attended.reshape(tok_rows, kv_local * query_group * head_size)
    terms = jnp.dot(
        attended,
        lax.all_gather(wo, ("seq", "srv"), axis=1, tiled=True),
        preferred_element_type=jnp.float32,
    )
    summed = lax.psum_scatter(
        terms.astype(jnp.bfloat16), "head", scatter_dimension=1, tiled=True
    ).astype(jnp.float32)
    return (source + summed).astype(jnp.bfloat16)


def solution(mesh):
    sizes = dict(mesh.shape)
    if sizes["grp"] == 1 and sizes["head"] == 1 and sizes["seq"] == 16 and sizes["srv"] == 2:
        fine = Mesh(np.asarray(mesh.devices).reshape(2, 2, 2, 2, 2), AXES)
        in_specs = (P(AXES), P(), P(AXES), P(AXES), P(AXES), P(None, AXES), P(AXES))
        return jax.shard_map(
            split_local, mesh=fine, in_specs=in_specs, out_specs=P(AXES), check_vma=False
        )
    in_specs = (
        P(("grp", "seq", "srv"), "head"),
        P(),
        P(("seq", "srv"), "head"),
        P(("seq", "srv"), "head"),
        P(("seq", "srv"), "head"),
        P("head", ("seq", "srv")),
        P(("grp", "seq", "srv")),
    )
    out_specs = P(("grp", "seq", "srv"), "head")
    return jax.shard_map(local, mesh=mesh, in_specs=in_specs, out_specs=out_specs, check_vma=False)
```

```python
import functools
import math

import jax
import jax.numpy as jnp
import numpy as np
from jax import lax
from jax.experimental import pallas as pl
from jax.experimental.pallas import tpu as pltpu
from jax.sharding import Mesh
from jax.sharding import PartitionSpec as P

QUERY_HEADS = 32
KV_HEAD_COUNT = 8
HEAD_WIDTH = 128
DOCS = 8


AXES = ("zh", "zl", "y", "x", "c")
QUAD = ("zl", "x", "c")
SWAP = [(0, 1), (1, 0)]
EXTRA = 16
QT = 256
KT = 512
NEG = -1e30

ANY = pl.BlockSpec(memory_space=pl.ANY)
VMEM = pl.BlockSpec(memory_space=pltpu.VMEM)
SMEM = pl.BlockSpec(memory_space=pltpu.SMEM)


def swap(value, axis):
    return lax.ppermute(value, axis, SWAP)


def after(value, *others):
    return lax.optimization_barrier((value, *others))[0]


def quad_gather(block, by_z_first):
    by_x = swap(block, "x")
    by_z = swap(block, "zl")
    far = swap(by_z, "x") if by_z_first else swap(by_x, "zl")
    got = {(0, 0): block, (0, 1): by_x, (1, 0): by_z, (1, 1): far}
    out = {}
    for (dzl, dx), piece in got.items():
        out[dzl, dx, 0] = piece
        out[dzl, dx, 1] = swap(piece, "c")
    return out


OFFSETS = [(dzl, dx, dc) for dzl in range(2) for dx in range(2) for dc in range(2)]


def start_copies(copies, sems, first=0):
    started = []
    for i, (src, dst) in enumerate(copies):
        copy = pltpu.make_async_copy(src, dst, sems.at[first + i])
        copy.start()
        started.append(copy)
    return started


def wait_all(copies):
    for copy in copies:
        copy.wait()


def aligned(value, step):
    return pl.multiple_of(value, step)


def project_kernel(where, *refs):
    tok_refs = dict(zip(OFFSETS, refs[:8]))
    wq_own, wq_y, wq_z0, wq_z1, wq_zy0, wq_zy1, wkv_near, wkv_far, cos_ref, sin_ref = refs[8:18]
    q_out, kv_out, xs, wq, wkv, sems = refs[18:]
    zh, zl, y, x, c = (where[i] for i in range(5))

    def rows_of(dzh, dy, zlp):
        return aligned((4 * (zh ^ dzh) + 2 * zlp + (y ^ dy)) * 512, 512)

    def token_copies(dzl):
        copies = []
        for dx in range(2):
            for dc in range(2):
                slot = 4 * (zl ^ dzl) + 2 * (x ^ dx) + (c ^ dc)
                dst = xs.at[pl.ds(aligned(slot * 128, 128), 128), :]
                copies.append((tok_refs[dzl, dx, dc], dst))
        return copies

    kv_copies = []
    for slot, (dzh, dy) in enumerate(((0, 0), (0, 1), (1, 0), (1, 1))):
        for j in range(8):
            src = wkv_far.at[j, pl.ds(0, 128), :]
            if slot < 3:
                src = wkv_near.at[j, pl.ds(slot * (128 + EXTRA), 128), :]
            row = aligned(rows_of(dzh, dy, j // 4) + (j % 4) * 128, 128)
            kv_copies.append((src, wkv.at[pl.ds(row, 128), :]))
    q_copies = []
    for zlp in range(2):
        for dzh, dy, src in (
            (0, 0, wq_own.at[pl.ds(zlp * 512, 512), :]),
            (0, 1, wq_y.at[pl.ds(zlp * 512, 512), :]),
            (1, 0, (wq_z0, wq_z1)[zlp]),
            (1, 1, (wq_zy0, wq_zy1)[zlp]),
        ):
            q_copies.append((src, wq.at[pl.ds(rows_of(dzh, dy, zlp), 512), :]))
    near = start_copies(token_copies(0), sems)
    near += start_copies(kv_copies, sems, 4)
    then = start_copies(q_copies, sems, 36)
    far = start_copies(token_copies(1), sems, 44)

    def turn(part, rows):
        return part * cos_ref[rows, :] + pltpu.roll(part, 64, axis=1) * sin_ref[rows, :]

    def rows_at(dzl):
        return pl.ds(aligned((zl ^ dzl) * 512, 512), 512)

    def kv_part(rows):
        acc = jnp.dot(xs[rows, :], wkv[...], preferred_element_type=jnp.float32)
        kv_out[rows, :128] = turn(acc[:, :128], rows).astype(jnp.bfloat16)
        kv_out[rows, 128:] = acc[:, 128:].astype(jnp.bfloat16)

    def q_part(rows):
        for n in range(2):
            acc = jnp.dot(
                xs[rows, :], wq[:, 256 * n : 256 * n + 256], preferred_element_type=jnp.float32
            )
            for k in range(2):
                columns = slice(256 * n + 128 * k, 256 * n + 128 * k + 128)
                part = acc[:, 128 * k : 128 * k + 128]
                q_out[rows, columns] = turn(part, rows).astype(jnp.bfloat16)

    wait_all(near)
    kv_part(rows_at(0))
    wait_all(then)
    q_part(rows_at(0))
    wait_all(far)
    kv_part(rows_at(1))
    q_part(rows_at(1))


FACTOR = math.log2(math.e) / math.sqrt(HEAD_WIDTH)


def first_position(zh, y, tile):
    return (2 * zh + tile // 2) * 1024 + y * 512 + (tile % 2) * QT


def copy_keys(kv_refs, y, ks, vs, sems):
    copies = []
    for dy, ref in enumerate(kv_refs):
        for zlp in range(2):
            row = aligned((2 * zlp + (y ^ dy)) * 512, 512)
            for half, dst in ((0, ks), (1, vs)):
                src = ref.at[pl.ds(zlp * 512, 512), pl.ds(half * 128, 128)]
                copies.append((src, dst.at[pl.ds(row, 512), :]))
    wait_all(start_copies(copies, sems))


def attend_step(queries, keys, values, state, mask):
    top, total, acc = state
    scores = lax.dot_general(
        queries, keys, (((1,), (1,)), ((), ())), preferred_element_type=jnp.float32
    )
    if mask is not None:
        scores = jnp.where(mask[None], scores.reshape(4, QT, KT), NEG).reshape(4 * QT, KT)
    cuts = [slice(128 * i, 128 * i + 128) for i in range(KT // 128)]
    best = functools.reduce(jnp.maximum, [scores[:, cut] for cut in cuts])
    old = top[...]
    new = jnp.maximum(old, jnp.max(best, axis=1, keepdims=True))
    top[...] = new
    shrink = jnp.exp2((old - new) * FACTOR)
    parts = [jnp.exp2((scores[:, cut] - new) * FACTOR) for cut in cuts]
    total[...] = total[...] * shrink + functools.reduce(jnp.add, parts)
    weights = jnp.concatenate([part.astype(jnp.bfloat16) for part in parts], axis=1)
    acc[...] = acc[...] * shrink + jnp.dot(weights, values, preferred_element_type=jnp.float32)


def stacked(q_ref):
    return jnp.concatenate([q_ref[:, 128 * h : 128 * h + 128] for h in range(4)], axis=0)


def near_kernel(where, tile_lo, tile_hi, q_ref, start_ref, kv_own, kv_y, *refs):
    top, total, acc, ks, vs, sems = refs
    zh, y = where[0], where[2]
    tile = pl.program_id(0)

    @pl.when(tile == 0)
    def _():
        copy_keys((kv_own, kv_y), y, ks, vs, sems)

    state = (top.at[0], total.at[0], acc.at[0])
    state[0][...] = jnp.full((4 * QT, 128), NEG, jnp.float32)
    state[1][...] = jnp.zeros((4 * QT, 128), jnp.float32)
    state[2][...] = jnp.zeros((4 * QT, 128), jnp.float32)
    first = first_position(zh, y, tile)
    base = zh * (2048 // KT)

    @pl.loop(jnp.maximum(tile_lo[tile] // KT, base), (first + QT + KT - 1) // KT)
    def _(block):
        keys = pl.ds(aligned((block - base) * KT, KT), KT)
        edge = (block * KT + KT - 1 > first) | (block * KT < tile_hi[tile])

        @pl.when(edge)
        def _():
            key_pos = block * KT + lax.broadcasted_iota(jnp.int32, (QT, KT), 1)
            query_pos = first + lax.broadcasted_iota(jnp.int32, (QT, KT), 0)
            mask = (key_pos <= query_pos) & (key_pos >= start_ref[:, :1])
            attend_step(stacked(q_ref), ks[keys, :], vs[keys, :], state, mask)

        @pl.when(jnp.logical_not(edge))
        def _():
            attend_step(stacked(q_ref), ks[keys, :], vs[keys, :], state, None)


def far_kernel(half, where, tile_lo, tile_hi, q_ref, start_ref, kv_z, kv_zy, *refs):
    top_in, total_in, acc_in, out_ref, ks, vs, top, total, acc, sems = refs
    zh, y = where[0], where[2]
    tile = 2 * half + pl.program_id(0)

    @pl.when((pl.program_id(0) == 0) & (zh == 1))
    def _():
        copy_keys((kv_z, kv_zy), y, ks, vs, sems)

    top[...] = top_in[0]
    total[...] = total_in[0]
    acc[...] = acc_in[0]

    @pl.loop(tile_lo[tile] // KT, zh * (2048 // KT))
    def _(block):
        keys = pl.ds(aligned(block * KT, KT), KT)
        edge = block * KT < tile_hi[tile]

        @pl.when(edge)
        def _():
            key_pos = block * KT + lax.broadcasted_iota(jnp.int32, (QT, KT), 1)
            mask = key_pos >= start_ref[:, :1]
            attend_step(stacked(q_ref), ks[keys, :], vs[keys, :], (top, total, acc), mask)

        @pl.when(jnp.logical_not(edge))
        def _():
            attend_step(stacked(q_ref), ks[keys, :], vs[keys, :], (top, total, acc), None)

    result = acc[...] / jnp.sum(total[...], axis=1, keepdims=True)
    for h in range(4):
        out_ref[:, 128 * h : 128 * h + 128] = result[QT * h : QT * h + QT].astype(jnp.bfloat16)


def output_kernel(with_first, where, *refs):
    att_refs = refs[:8]
    wo_refs = refs[8:16]
    rest = refs[16:]
    out_ref, xs, wo, sems = rest[-4:]
    zh, zl, y, x, c = (where[i] for i in range(5))
    copies = []
    for (dzl, dx, dc), ref in zip(OFFSETS, att_refs):
        slot = 4 * (zl ^ dzl) + 2 * (x ^ dx) + (c ^ dc)
        copies.append((ref, xs.at[:, pl.ds(aligned(slot * 512, 512), 512)]))
    for i, ref in enumerate(wo_refs):
        column = aligned((2 * (zh ^ (i // 2 % 2)) + (y ^ (i % 2))) * 128, 128)
        copies.append((ref, wo.at[2048 * (i // 4) : 2048 * (i // 4) + 2048, pl.ds(column, 128)]))
    started = start_copies(copies, sems)
    base = 0
    if with_first:
        base = 512
        out_ref[:512, :] = rest[0][...]
    wait_all(started)
    for n in range(2):
        columns = slice(256 * n, 256 * n + 256)
        acc = jnp.dot(xs[...], wo[:, columns], preferred_element_type=jnp.float32)
        out_ref[base : base + 512, columns] = acc.astype(jnp.bfloat16)


def finish_kernel(tok_ref, sent_ref, out_ref):
    for block in range(32):
        zhp, zlp, yp, xp, cp = ((block >> s) & 1 for s in (4, 3, 2, 1, 0))
        source, part = 4 * zlp + 2 * xp + cp, 2 * zhp + yp
        columns = slice(128 * block, 128 * block + 128)
        sent = sent_ref[source, :, 128 * part : 128 * part + 128].astype(jnp.float32)
        out_ref[:, columns] = (tok_ref[:, columns].astype(jnp.float32) + sent).astype(jnp.bfloat16)


def call(kernel, out_shape, in_specs, scratch, cost, **more):
    flops, moved = cost
    more.setdefault("out_specs", jax.tree.map(lambda _: VMEM, out_shape))
    return pl.pallas_call(
        kernel,
        out_shape=out_shape,
        in_specs=in_specs,
        scratch_shapes=scratch,
        compiler_params=pltpu.CompilerParams(vmem_limit_bytes=48 * 1024 * 1024),
        cost_estimate=pl.CostEstimate(flops=flops, bytes_accessed=moved, transcendentals=0),
        **more,
    )


def split_body(tokens, norm_gain, wq, wk, wv, wo, doc_ids):
    bf16, f32 = jnp.bfloat16, jnp.float32
    zh, zl, y, x, c = place = [lax.axis_index(axis) for axis in AXES]
    where = jnp.stack(place).astype(jnp.int32)

    below = jnp.sum(
        doc_ids[:, None] < lax.broadcasted_iota(jnp.int32, (1, 256), 1), axis=0, dtype=jnp.int32
    ).astype(bf16)
    wkv = jnp.concatenate([wk.reshape(128, 8, 128), wv.reshape(128, 8, 128)], axis=2)
    wkv = jnp.concatenate([wkv, jnp.broadcast_to(below, (EXTRA, 8, 256))], axis=0)
    wkv = jnp.transpose(wkv, (1, 0, 2))
    wkv_z = swap(wkv, "zh")
    wkv_y = swap(wkv, "y")

    wqs = jnp.transpose(wq.reshape(128, 8, 512), (1, 0, 2))
    wqs = lax.all_to_all(wqs, QUAD, 0, 0, tiled=True).reshape(1024, 512)
    wq_z0 = swap(wqs[:512], "zh")
    wq_z1 = swap(wqs[512:], "zh")
    wq_y = swap(wqs, "y")
    wq_zy0 = swap(wq_z0, "y")
    wq_zy1 = swap(wq_z1, "y")

    near = jnp.concatenate([wkv, wkv_y, wkv_z], axis=1)
    near = lax.all_to_all(near, QUAD, 0, 0, tiled=True)
    far = swap(near[:, 2 * (128 + EXTRA) :], "y")

    source = tokens.astype(f32)
    mean_sq = jnp.mean(source * source, axis=1, keepdims=True)
    normed = (source * lax.rsqrt(mean_sq + 1e-05) * norm_gain[None, :]).astype(bf16)
    tok = quad_gather(after(normed, wqs), True)

    token = jnp.arange(1024, dtype=jnp.int32)
    positions = (2 * zh + token // 512) * 1024 + y * 512 + token % 512
    freqs = 500000.0 ** (-(jnp.arange(64, dtype=f32) * 2.0 / HEAD_WIDTH))
    angles = positions.astype(f32)[:, None] * freqs[None, :]
    cosine, sine = jnp.cos(angles), jnp.sin(angles)
    cosine = jnp.concatenate([cosine, cosine], axis=1)
    sine = jnp.concatenate([-sine, sine], axis=1)

    counts = [near[:, 128 + i * (128 + EXTRA), :DOCS] for i in range(3)] + [far[:, 128, :DOCS]]
    starts = jnp.sum(jnp.concatenate(counts, axis=0).astype(f32), axis=0).astype(jnp.int32)
    query_start = jnp.max(
        jnp.where(positions[:, None] >= starts[None, :], starts[None, :], 0), axis=1
    )
    tile_lo = query_start[::QT]
    tile_hi = query_start[QT - 1 :: QT]
    start_col = jnp.broadcast_to(query_start[:, None], (1024, 128))

    queries, keys_values = call(
        project_kernel,
        (
            jax.ShapeDtypeStruct((1024, 512), bf16),
            jax.ShapeDtypeStruct((1024, 256), bf16),
        ),
        [SMEM] + [ANY] * 16 + [VMEM, VMEM],
        [
            pltpu.VMEM((1024, 4096), bf16),
            pltpu.VMEM((4096, 512), bf16),
            pltpu.VMEM((4096, 256), bf16),
            pltpu.SemaphoreType.DMA((48,)),
        ],
        (2 * 1024 * 4096 * 768, 17 << 20),
    )(
        where, *[tok[at] for at in OFFSETS],
        wqs, wq_y, wq_z0, wq_z1, wq_zy0, wq_zy1, near, far, cosine, sine,
    )

    kv_y = swap(keys_values, "y")
    kv_z = swap(keys_values, "zh")
    kv_zy = swap(kv_z, "y")

    def tile_spec(shape, first):
        return pl.BlockSpec(shape, lambda i: (i + first,) + (0,) * (len(shape) - 1))

    def state_specs(first):
        return [tile_spec((1, 4 * QT, 128), first)] * 3

    state = call(
        near_kernel,
        [jax.ShapeDtypeStruct((4, 4 * QT, 128), f32)] * 3,
        [SMEM, SMEM, SMEM, tile_spec((QT, 512), 0), tile_spec((QT, 128), 0), ANY, ANY],
        [
            pltpu.VMEM((2048, 128), bf16),
            pltpu.VMEM((2048, 128), bf16),
            pltpu.SemaphoreType.DMA((8,)),
        ],
        (4 * 1024 * 2048 * 512, 8 << 20),
        grid=(4,),
        out_specs=state_specs(0),
    )(where, tile_lo, tile_hi, queries, start_col, keys_values, kv_y)

    def far_call(half):
        return call(
            functools.partial(far_kernel, half),
            jax.ShapeDtypeStruct((512, 512), bf16),
            [SMEM, SMEM, SMEM, tile_spec((QT, 512), 2 * half), tile_spec((QT, 128), 2 * half)]
            + [ANY, ANY] + state_specs(2 * half),
            [
                pltpu.VMEM((2048, 128), bf16),
                pltpu.VMEM((2048, 128), bf16),
                pltpu.VMEM((4 * QT, 128), f32),
                pltpu.VMEM((4 * QT, 128), f32),
                pltpu.VMEM((4 * QT, 128), f32),
                pltpu.SemaphoreType.DMA((8,)),
            ],
            (4 * 512 * 2048 * 512, 8 << 20),
            grid=(2,),
            out_specs=pl.BlockSpec((QT, 512), lambda i: (i, 0)),
        )(where, tile_lo, tile_hi, queries, start_col, kv_z, kv_zy, *state)

    attended = [far_call(0), far_call(1)]

    wos = []
    for part in range(2):
        piece = wo[2048 * part : 2048 * part + 2048]
        by_z = swap(piece, "zh")
        wos += [piece, swap(piece, "y"), by_z, swap(by_z, "y")]

    def output(half, first):
        att = quad_gather(attended[half], half == 1)
        rows = 1024 if first else 512
        return call(
            functools.partial(output_kernel, bool(first)),
            jax.ShapeDtypeStruct((rows, 512), bf16),
            [SMEM] + [ANY] * 16 + [VMEM] * len(first),
            [
                pltpu.VMEM((512, 4096), bf16),
                pltpu.VMEM((4096, 512), bf16),
                pltpu.SemaphoreType.DMA((16,)),
            ],
            (2 * 512 * 4096 * 512, 9 << 20),
        )(where, *[att[at] for at in OFFSETS], *wos, *first)

    sent = output(1, [output(0, [])])
    home = lax.all_to_all(sent.reshape(8, 128, 512), QUAD, 0, 0, tiled=True)
    return call(
        finish_kernel,
        jax.ShapeDtypeStruct((128, 4096), bf16),
        [VMEM, VMEM],
        [],
        (128 * 4096, 3 << 20),
    )(tokens, home)


def rope(field, positions):
    half = field.shape[-1] // 2
    freqs = 500000.0 ** (-(jnp.arange(half, dtype=jnp.float32) * 2.0 / field.shape[-1]))
    angles = positions.astype(jnp.float32)[:, None] * freqs[None, :]
    cosine = jnp.cos(angles)[:, None, :]
    sine = jnp.sin(angles)[:, None, :]
    first = field[..., :half]
    second = field[..., half:]
    return jnp.concatenate(
        [first * cosine - second * sine, second * cosine + first * sine], axis=-1
    )


def local(tokens, norm_gain, wq, wk, wv, wo, doc_ids):
    tok_rows = tokens.shape[0]
    head_size = HEAD_WIDTH
    kv_local = wk.shape[1] // head_size
    query_group = QUERY_HEADS // KV_HEAD_COUNT
    source = tokens.astype(jnp.float32)
    whole = lax.all_gather(tokens, "head", axis=1, tiled=True).astype(jnp.float32)
    mean_sq = jnp.mean(whole * whole, axis=1, keepdims=True)
    normed_input = (whole * lax.rsqrt(mean_sq + 1e-05) * norm_gain[None, :]).astype(jnp.bfloat16)
    query_acc = jnp.dot(
        normed_input,
        lax.all_gather(wq, ("seq", "srv"), axis=0, tiled=True),
        preferred_element_type=jnp.float32,
    )
    key_acc = jnp.dot(
        normed_input,
        lax.all_gather(wk, ("seq", "srv"), axis=0, tiled=True),
        preferred_element_type=jnp.float32,
    )
    value_acc = jnp.dot(
        normed_input,
        lax.all_gather(wv, ("seq", "srv"), axis=0, tiled=True),
        preferred_element_type=jnp.float32,
    )
    first_pos = lax.axis_index(("seq", "srv")) * tok_rows
    positions = first_pos + jnp.arange(tok_rows, dtype=jnp.int32)
    query_matrix = rope(query_acc.reshape(tok_rows, kv_local * query_group, head_size), positions)
    query_matrix = query_matrix.astype(jnp.bfloat16).reshape(
        tok_rows, kv_local, query_group, head_size
    )
    key_matrix = rope(key_acc.reshape(tok_rows, kv_local, head_size), positions).astype(
        jnp.bfloat16
    )
    key_matrix = key_matrix.reshape(tok_rows, kv_local * head_size)
    value_matrix = value_acc.astype(jnp.bfloat16)
    scale = 1.0 / head_size**0.5

    def attend_block(carry, key_rows, value_rows, doc_rows, key_pos):
        run_top, run_total, run_acc = carry
        key_heads = key_rows.reshape(key_rows.shape[0], kv_local, head_size)
        value_heads = value_rows.reshape(value_rows.shape[0], kv_local, head_size)
        scores = (
            jnp.einsum(
                "qcgd,kcd->qcgk", query_matrix, key_heads, preferred_element_type=jnp.float32
            )
            * scale
        )
        allowed = (
            (key_pos[None, :] <= positions[:, None])
            & (key_pos[None, :] >= 0)
            & (doc_rows[None, :] == doc_ids[:, None])
        )
        allowed = allowed[:, None, None, :]
        masked = jnp.where(allowed, scores, -1e30)
        new_top = jnp.maximum(run_top, jnp.max(masked, axis=3))
        expd = jnp.where(allowed, jnp.exp(masked - new_top[..., None]), 0.0)
        factor = jnp.exp(run_top - new_top)
        new_total = run_total * factor + jnp.sum(expd, axis=3)
        weights = expd.astype(jnp.bfloat16)
        update = jnp.einsum(
            "qcgk,kcd->qcgd", weights, value_heads, preferred_element_type=jnp.float32
        )
        return (new_top, new_total, run_acc * factor[..., None] + update)

    start_state = (
        jnp.full((tok_rows, kv_local, query_group), -1e30, jnp.float32),
        jnp.zeros((tok_rows, kv_local, query_group), jnp.float32),
        jnp.zeros((tok_rows, kv_local, query_group, head_size), jnp.float32),
    )
    key_piece = lax.all_gather(key_matrix, ("seq", "srv"), axis=0, tiled=True)
    value_piece = lax.all_gather(value_matrix, ("seq", "srv"), axis=0, tiled=True)
    doc_piece = lax.all_gather(doc_ids, ("seq", "srv"), axis=0, tiled=True)
    count = key_piece.shape[0]
    width = math.gcd(count, 512)

    def step(inner, index):
        offset = index * width
        key_rows = lax.dynamic_slice_in_dim(key_piece, offset, width, 0)
        value_rows = lax.dynamic_slice_in_dim(value_piece, offset, width, 0)
        doc_rows = lax.dynamic_slice_in_dim(doc_piece, offset, width, 0)
        key_pos = offset + jnp.arange(width, dtype=jnp.int32)
        return (attend_block(inner, key_rows, value_rows, doc_rows, key_pos), None)

    def run_all(inner):
        result, _ = lax.scan(step, inner, jnp.arange(count // width, dtype=jnp.int32))
        return result

    beyond = jnp.int32(0) > first_pos + tok_rows - 1
    before = doc_piece[count - 1] < doc_ids[0]
    _, final_total, final_acc = lax.cond(beyond | before, lambda inner: inner, run_all, start_state)
    attended = (final_acc / final_total[..., None]).astype(jnp.bfloat16)
    attended = attended.reshape(tok_rows, kv_local * query_group * head_size)
    terms = jnp.dot(
        attended,
        lax.all_gather(wo, ("seq", "srv"), axis=1, tiled=True),
        preferred_element_type=jnp.float32,
    )
    summed = lax.psum_scatter(
        terms.astype(jnp.bfloat16), "head", scatter_dimension=1, tiled=True
    ).astype(jnp.float32)
    return (source + summed).astype(jnp.bfloat16)


def solution(mesh):
    sizes = dict(mesh.shape)
    if sizes["grp"] == 1 and sizes["head"] == 1 and sizes["seq"] == 16 and sizes["srv"] == 2:
        fine = Mesh(np.asarray(mesh.devices).reshape(2, 2, 2, 2, 2), AXES)
        in_specs = (P(AXES), P(), P(AXES), P(AXES), P(AXES), P(None, AXES), P(AXES))
        return jax.shard_map(
            split_body, mesh=fine, in_specs=in_specs, out_specs=P(AXES), check_vma=False
        )
    in_specs = (
        P(("grp", "seq", "srv"), "head"),
        P(),
        P(("seq", "srv"), "head"),
        P(("seq", "srv"), "head"),
        P(("seq", "srv"), "head"),
        P("head", ("seq", "srv")),
        P(("grp", "seq", "srv")),
    )
    out_specs = P(("grp", "seq", "srv"), "head")
    return jax.shard_map(local, mesh=mesh, in_specs=in_specs, out_specs=out_specs, check_vma=False)
```

```python
import functools
import math

import jax
import jax.numpy as jnp
import numpy as np
from jax import lax
from jax.experimental import pallas as pl
from jax.experimental.pallas import tpu as pltpu
from jax.sharding import Mesh
from jax.sharding import PartitionSpec as P

QUERY_HEADS = 32
KV_HEAD_COUNT = 8
HEAD_WIDTH = 128
DOCS = 8


AXES = ("zh", "zl", "y", "x", "c")
QUAD = ("zl", "x", "c")
SWAP = [(0, 1), (1, 0)]
EXTRA = 16
QT = 256
KT = 512
NEG = -1e30

ANY = pl.BlockSpec(memory_space=pl.ANY)
VMEM = pl.BlockSpec(memory_space=pltpu.VMEM)
SMEM = pl.BlockSpec(memory_space=pltpu.SMEM)


def swap(value, axis):
    return lax.ppermute(value, axis, SWAP)


def after(value, *others):
    return lax.optimization_barrier((value, *others))[0]


def quad_gather(block, by_z_first):
    by_x = swap(block, "x")
    by_z = swap(block, "zl")
    far = swap(by_z, "x") if by_z_first else swap(by_x, "zl")
    got = {(0, 0): block, (0, 1): by_x, (1, 0): by_z, (1, 1): far}
    out = {}
    for (dzl, dx), piece in got.items():
        out[dzl, dx, 0] = piece
        out[dzl, dx, 1] = swap(piece, "c")
    return out


OFFSETS = [(dzl, dx, dc) for dzl in range(2) for dx in range(2) for dc in range(2)]


def start_copies(copies, sems, first=0):
    started = []
    for i, (src, dst) in enumerate(copies):
        copy = pltpu.make_async_copy(src, dst, sems.at[first + i])
        copy.start()
        started.append(copy)
    return started


def wait_all(copies):
    for copy in copies:
        copy.wait()


def aligned(value, step):
    return pl.multiple_of(value, step)


TOKEN_PIECES = [
    (dzl, dx, dc, first, rows)
    for dzl, dx, first, rows in (
        (0, 0, 0, 128),
        (0, 1, 0, 128),
        (1, 0, 0, 64),
        (1, 0, 64, 64),
        (1, 1, 0, 64),
        (1, 1, 64, 64),
    )
    for dc in range(2)
]


def token_copies(dzl, where, tok_refs, xs):
    zl, x, c = where[1], where[3], where[4]
    copies = []
    for (piece_dzl, dx, dc, first, rows), ref in zip(TOKEN_PIECES, tok_refs):
        if piece_dzl == dzl:
            slot = 4 * (zl ^ dzl) + 2 * (x ^ dx) + (c ^ dc)
            copies.append((ref, xs.at[pl.ds(aligned(slot * 128 + first, 64), rows), :]))
    return copies


def weight_row(where, dzh, dy, zlp):
    return aligned((4 * (where[0] ^ dzh) + 2 * zlp + (where[2] ^ dy)) * 512, 512)


def turn(part, cos_ref, sin_ref, rows):
    return part * cos_ref[rows, :] + pltpu.roll(part, 64, axis=1) * sin_ref[rows, :]


def project_kv_kernel(where, *refs):
    tok_refs, wkv_refs, (cos_ref, sin_ref) = refs[:12], refs[12:16], refs[16:18]
    kv_out, xs, wkv, sems = refs[18:]
    copies = []
    for (dzh, dy), ref in zip(((0, 0), (0, 1), (1, 0), (1, 1)), wkv_refs):
        for j in range(8):
            row = aligned(weight_row(where, dzh, dy, j // 4) + (j % 4) * 128, 128)
            copies.append((ref.at[j, pl.ds(0, 128), :], wkv.at[pl.ds(row, 128), :]))
    near = start_copies(token_copies(0, where, tok_refs, xs), sems)
    near += start_copies(copies, sems, 4)
    far = start_copies(token_copies(1, where, tok_refs, xs), sems, 36)
    for dzl, waits in enumerate((near, far)):
        wait_all(waits)
        rows = pl.ds(aligned((where[1] ^ dzl) * 512, 512), 512)
        acc = jnp.dot(xs[rows, :], wkv[...], preferred_element_type=jnp.float32)
        kv_out[rows, :128] = turn(acc[:, :128], cos_ref, sin_ref, rows).astype(jnp.bfloat16)
        kv_out[rows, 128:] = acc[:, 128:].astype(jnp.bfloat16)


def project_q_kernel(where, *refs):
    tok_refs = refs[:12]
    wq_own, wq_y, wq_z0, wq_z1, wq_zy0, wq_zy1, cos_ref, sin_ref = refs[12:20]
    q_out, xs, wq, sems = refs[20:]
    copies = []
    for zlp in range(2):
        for dzh, dy, src in (
            (0, 0, wq_own.at[pl.ds(zlp * 512, 512), :]),
            (0, 1, wq_y.at[pl.ds(zlp * 512, 512), :]),
            (1, 0, (wq_z0, wq_z1)[zlp]),
            (1, 1, (wq_zy0, wq_zy1)[zlp]),
        ):
            copies.append((src, wq.at[pl.ds(weight_row(where, dzh, dy, zlp), 512), :]))
    near = start_copies(token_copies(0, where, tok_refs, xs), sems)
    near += start_copies(copies, sems, 4)
    far = start_copies(token_copies(1, where, tok_refs, xs), sems, 12)
    for dzl, waits in enumerate((near, far)):
        wait_all(waits)
        rows = pl.ds(aligned((where[1] ^ dzl) * 512, 512), 512)
        for n in range(2):
            acc = jnp.dot(
                xs[rows, :], wq[:, 256 * n : 256 * n + 256], preferred_element_type=jnp.float32
            )
            for k in range(2):
                part = turn(acc[:, 128 * k : 128 * k + 128], cos_ref, sin_ref, rows)
                columns = slice(256 * n + 128 * k, 256 * n + 128 * k + 128)
                q_out[rows, columns] = part.astype(jnp.bfloat16)


FACTOR = math.log2(math.e) / math.sqrt(HEAD_WIDTH)


def first_position(zh, y, tile):
    return (2 * zh + tile // 2) * 1024 + y * 512 + (tile % 2) * QT


def copy_keys(kv_refs, y, ks, vs, sems):
    copies = []
    for dy, ref in enumerate(kv_refs):
        for zlp in range(2):
            row = aligned((2 * zlp + (y ^ dy)) * 512, 512)
            for half, dst in ((0, ks), (1, vs)):
                src = ref.at[pl.ds(zlp * 512, 512), pl.ds(half * 128, 128)]
                copies.append((src, dst.at[pl.ds(row, 512), :]))
    wait_all(start_copies(copies, sems))


def attend_step(queries, keys, values, state, mask):
    top, total, acc = state
    scores = lax.dot_general(
        queries, keys, (((1,), (1,)), ((), ())), preferred_element_type=jnp.float32
    )
    if mask is not None:
        scores = jnp.where(mask[None], scores.reshape(4, QT, KT), NEG).reshape(4 * QT, KT)
    cuts = [slice(128 * i, 128 * i + 128) for i in range(KT // 128)]
    best = functools.reduce(jnp.maximum, [scores[:, cut] for cut in cuts])
    old = top[...]
    new = jnp.maximum(old, jnp.max(best, axis=1, keepdims=True))
    top[...] = new
    shrink = jnp.exp2((old - new) * FACTOR)
    parts = [jnp.exp2((scores[:, cut] - new) * FACTOR) for cut in cuts]
    total[...] = total[...] * shrink + functools.reduce(jnp.add, parts)
    weights = jnp.concatenate([part.astype(jnp.bfloat16) for part in parts], axis=1)
    acc[...] = acc[...] * shrink + jnp.dot(weights, values, preferred_element_type=jnp.float32)


def stacked(q_ref):
    return jnp.concatenate([q_ref[:, 128 * h : 128 * h + 128] for h in range(4)], axis=0)


def near_kernel(where, tile_lo, tile_hi, q_ref, start_ref, kv_own, kv_y, *refs):
    top, total, acc, ks, vs, sems = refs
    zh, y = where[0], where[2]
    tile = pl.program_id(0)

    @pl.when(tile == 0)
    def _():
        copy_keys((kv_own, kv_y), y, ks, vs, sems)

    state = (top.at[0], total.at[0], acc.at[0])
    state[0][...] = jnp.full((4 * QT, 128), NEG, jnp.float32)
    state[1][...] = jnp.zeros((4 * QT, 128), jnp.float32)
    state[2][...] = jnp.zeros((4 * QT, 128), jnp.float32)
    first = first_position(zh, y, tile)
    base = zh * (2048 // KT)

    @pl.loop(jnp.maximum(tile_lo[tile] // KT, base), (first + QT + KT - 1) // KT)
    def _(block):
        keys = pl.ds(aligned((block - base) * KT, KT), KT)
        edge = (block * KT + KT - 1 > first) | (block * KT < tile_hi[tile])

        @pl.when(edge)
        def _():
            key_pos = block * KT + lax.broadcasted_iota(jnp.int32, (QT, KT), 1)
            query_pos = first + lax.broadcasted_iota(jnp.int32, (QT, KT), 0)
            mask = (key_pos <= query_pos) & (key_pos >= start_ref[:, :1])
            attend_step(stacked(q_ref), ks[keys, :], vs[keys, :], state, mask)

        @pl.when(jnp.logical_not(edge))
        def _():
            attend_step(stacked(q_ref), ks[keys, :], vs[keys, :], state, None)


def far_kernel(half, where, tile_lo, tile_hi, q_ref, start_ref, kv_z, kv_zy, *refs):
    top_in, total_in, acc_in, out_ref, ks, vs, top, total, acc, sems = refs
    zh, y = where[0], where[2]
    tile = 2 * half + pl.program_id(0)

    @pl.when((pl.program_id(0) == 0) & (zh == 1))
    def _():
        copy_keys((kv_z, kv_zy), y, ks, vs, sems)

    top[...] = top_in[0]
    total[...] = total_in[0]
    acc[...] = acc_in[0]

    @pl.loop(tile_lo[tile] // KT, zh * (2048 // KT))
    def _(block):
        keys = pl.ds(aligned(block * KT, KT), KT)
        edge = block * KT < tile_hi[tile]

        @pl.when(edge)
        def _():
            key_pos = block * KT + lax.broadcasted_iota(jnp.int32, (QT, KT), 1)
            mask = key_pos >= start_ref[:, :1]
            attend_step(stacked(q_ref), ks[keys, :], vs[keys, :], (top, total, acc), mask)

        @pl.when(jnp.logical_not(edge))
        def _():
            attend_step(stacked(q_ref), ks[keys, :], vs[keys, :], (top, total, acc), None)

    result = acc[...] / jnp.sum(total[...], axis=1, keepdims=True)
    for h in range(4):
        out_ref[:, 128 * h : 128 * h + 128] = result[QT * h : QT * h + QT].astype(jnp.bfloat16)


def output_kernel(with_first, where, *refs):
    att_refs = refs[:8]
    wo_refs = refs[8:16]
    rest = refs[16:]
    out_ref, xs, wo, sems = rest[-4:]
    zh, zl, y, x, c = (where[i] for i in range(5))
    copies = []
    for (dzl, dx, dc), ref in zip(OFFSETS, att_refs):
        slot = 4 * (zl ^ dzl) + 2 * (x ^ dx) + (c ^ dc)
        copies.append((ref, xs.at[:, pl.ds(aligned(slot * 512, 512), 512)]))
    for i, ref in enumerate(wo_refs):
        column = aligned((2 * (zh ^ (i // 2 % 2)) + (y ^ (i % 2))) * 128, 128)
        copies.append((ref, wo.at[2048 * (i // 4) : 2048 * (i // 4) + 2048, pl.ds(column, 128)]))
    started = start_copies(copies, sems)
    base = 0
    if with_first:
        base = 512
        out_ref[:512, :] = rest[0][...]
    wait_all(started)
    for n in range(2):
        columns = slice(256 * n, 256 * n + 256)
        acc = jnp.dot(xs[...], wo[:, columns], preferred_element_type=jnp.float32)
        out_ref[base : base + 512, columns] = acc.astype(jnp.bfloat16)


def finish_kernel(tok_ref, sent_ref, out_ref):
    for block in range(32):
        zhp, zlp, yp, xp, cp = ((block >> s) & 1 for s in (4, 3, 2, 1, 0))
        source, part = 4 * zlp + 2 * xp + cp, 2 * zhp + yp
        columns = slice(128 * block, 128 * block + 128)
        sent = sent_ref[source, :, 128 * part : 128 * part + 128].astype(jnp.float32)
        out_ref[:, columns] = (tok_ref[:, columns].astype(jnp.float32) + sent).astype(jnp.bfloat16)


def call(kernel, out_shape, in_specs, scratch, cost, **more):
    flops, moved = cost
    more.setdefault("out_specs", jax.tree.map(lambda _: VMEM, out_shape))
    return pl.pallas_call(
        kernel,
        out_shape=out_shape,
        in_specs=in_specs,
        scratch_shapes=scratch,
        compiler_params=pltpu.CompilerParams(vmem_limit_bytes=48 * 1024 * 1024),
        cost_estimate=pl.CostEstimate(flops=flops, bytes_accessed=moved, transcendentals=0),
        **more,
    )


def split_body(tokens, norm_gain, wq, wk, wv, wo, doc_ids):
    bf16, f32 = jnp.bfloat16, jnp.float32
    zh, zl, y, x, c = place = [lax.axis_index(axis) for axis in AXES]
    where = jnp.stack(place).astype(jnp.int32)

    below = jnp.sum(
        doc_ids[:, None] < lax.broadcasted_iota(jnp.int32, (1, 256), 1), axis=0, dtype=jnp.int32
    ).astype(bf16)
    wkv = jnp.concatenate([wk.reshape(128, 8, 128), wv.reshape(128, 8, 128)], axis=2)
    wkv = jnp.concatenate([wkv, jnp.broadcast_to(below, (EXTRA, 8, 256))], axis=0)
    wkv = lax.all_to_all(jnp.transpose(wkv, (1, 0, 2)), QUAD, 0, 0, tiled=True)
    wkv_z = swap(wkv, "zh")
    wkvs = [wkv, swap(wkv, "y"), wkv_z, swap(wkv_z, "y")]

    wqs = jnp.transpose(wq.reshape(128, 8, 512), (1, 0, 2))
    wqs = lax.all_to_all(after(wqs, wkv), QUAD, 0, 0, tiled=True).reshape(1024, 512)
    wq_z0 = swap(wqs[:512], "zh")
    wq_z1 = swap(wqs[512:], "zh")
    wq_y = swap(wqs, "y")
    wq_zy0 = swap(wq_z0, "y")
    wq_zy1 = swap(wq_z1, "y")

    source = tokens.astype(f32)
    mean_sq = jnp.mean(source * source, axis=1, keepdims=True)
    normed = (source * lax.rsqrt(mean_sq + 1e-05) * norm_gain[None, :]).astype(bf16)
    normed = after(normed, wqs)
    tok_z = [swap(normed[64 * i : 64 * i + 64], "zl") for i in range(2)]
    tok_far = [swap(tok_z[i], "x") for i in range(2)]
    tok = []
    for piece in [normed, swap(normed, "x"), *tok_z, *tok_far]:
        tok += [piece, swap(piece, "c")]

    token = jnp.arange(1024, dtype=jnp.int32)
    positions = (2 * zh + token // 512) * 1024 + y * 512 + token % 512
    freqs = 500000.0 ** (-(jnp.arange(64, dtype=f32) * 2.0 / HEAD_WIDTH))
    angles = positions.astype(f32)[:, None] * freqs[None, :]
    cosine, sine = jnp.cos(angles), jnp.sin(angles)
    cosine = jnp.concatenate([cosine, cosine], axis=1)
    sine = jnp.concatenate([-sine, sine], axis=1)

    counts = jnp.concatenate([piece[:, 128, :DOCS] for piece in wkvs], axis=0)
    starts = jnp.sum(counts.astype(f32), axis=0).astype(jnp.int32)
    query_start = jnp.max(
        jnp.where(positions[:, None] >= starts[None, :], starts[None, :], 0), axis=1
    )
    tile_lo = query_start[::QT]
    tile_hi = query_start[QT - 1 :: QT]
    start_col = jnp.broadcast_to(query_start[:, None], (1024, 128))

    keys_values = call(
        project_kv_kernel,
        jax.ShapeDtypeStruct((1024, 256), bf16),
        [SMEM] + [ANY] * 16 + [VMEM, VMEM],
        [
            pltpu.VMEM((1024, 4096), bf16),
            pltpu.VMEM((4096, 256), bf16),
            pltpu.SemaphoreType.DMA((44,)),
        ],
        (2 * 1024 * 4096 * 256, 11 << 20),
    )(where, *tok, *wkvs, cosine, sine)
    queries = call(
        project_q_kernel,
        jax.ShapeDtypeStruct((1024, 512), bf16),
        [SMEM] + [ANY] * 18 + [VMEM, VMEM],
        [
            pltpu.VMEM((1024, 4096), bf16),
            pltpu.VMEM((4096, 512), bf16),
            pltpu.SemaphoreType.DMA((20,)),
        ],
        (2 * 1024 * 4096 * 512, 14 << 20),
    )(where, *tok, wqs, wq_y, wq_z0, wq_z1, wq_zy0, wq_zy1, cosine, sine)

    kv_y = swap(keys_values, "y")
    kv_z = swap(keys_values, "zh")
    kv_zy = swap(kv_z, "y")

    def tile_spec(shape, first):
        return pl.BlockSpec(shape, lambda i: (i + first,) + (0,) * (len(shape) - 1))

    def state_specs(first):
        return [tile_spec((1, 4 * QT, 128), first)] * 3

    state = call(
        near_kernel,
        [jax.ShapeDtypeStruct((4, 4 * QT, 128), f32)] * 3,
        [SMEM, SMEM, SMEM, tile_spec((QT, 512), 0), tile_spec((QT, 128), 0), ANY, ANY],
        [
            pltpu.VMEM((2048, 128), bf16),
            pltpu.VMEM((2048, 128), bf16),
            pltpu.SemaphoreType.DMA((8,)),
        ],
        (4 * 1024 * 2048 * 512, 8 << 20),
        grid=(4,),
        out_specs=state_specs(0),
    )(where, tile_lo, tile_hi, queries, start_col, keys_values, kv_y)

    def far_call(half):
        return call(
            functools.partial(far_kernel, half),
            jax.ShapeDtypeStruct((512, 512), bf16),
            [SMEM, SMEM, SMEM, tile_spec((QT, 512), 2 * half), tile_spec((QT, 128), 2 * half)]
            + [ANY, ANY] + state_specs(2 * half),
            [
                pltpu.VMEM((2048, 128), bf16),
                pltpu.VMEM((2048, 128), bf16),
                pltpu.VMEM((4 * QT, 128), f32),
                pltpu.VMEM((4 * QT, 128), f32),
                pltpu.VMEM((4 * QT, 128), f32),
                pltpu.SemaphoreType.DMA((8,)),
            ],
            (4 * 512 * 2048 * 512, 8 << 20),
            grid=(2,),
            out_specs=pl.BlockSpec((QT, 512), lambda i: (i, 0)),
        )(where, tile_lo, tile_hi, queries, start_col, kv_z, kv_zy, *state)

    attended = [far_call(0), far_call(1)]

    wos = []
    for part in range(2):
        piece = wo[2048 * part : 2048 * part + 2048]
        by_z = swap(piece, "zh")
        wos += [piece, swap(piece, "y"), by_z, swap(by_z, "y")]

    def output(half, first):
        att = quad_gather(attended[half], half == 1)
        rows = 1024 if first else 512
        return output_call(att, first, rows)

    def output_call(att, first, rows):
        return call(
            functools.partial(output_kernel, bool(first)),
            jax.ShapeDtypeStruct((rows, 512), bf16),
            [SMEM] + [ANY] * 16 + [VMEM] * len(first),
            [
                pltpu.VMEM((512, 4096), bf16),
                pltpu.VMEM((4096, 512), bf16),
                pltpu.SemaphoreType.DMA((16,)),
            ],
            (2 * 512 * 4096 * 512, 9 << 20),
        )(where, *[att[at] for at in OFFSETS], *wos, *first)

    sent = output(1, [output(0, [])])
    home = lax.all_to_all(sent.reshape(8, 128, 512), QUAD, 0, 0, tiled=True)
    return call(
        finish_kernel,
        jax.ShapeDtypeStruct((128, 4096), bf16),
        [VMEM, VMEM],
        [],
        (128 * 4096, 3 << 20),
    )(tokens, home)


def rope(field, positions):
    half = field.shape[-1] // 2
    freqs = 500000.0 ** (-(jnp.arange(half, dtype=jnp.float32) * 2.0 / field.shape[-1]))
    angles = positions.astype(jnp.float32)[:, None] * freqs[None, :]
    cosine = jnp.cos(angles)[:, None, :]
    sine = jnp.sin(angles)[:, None, :]
    first = field[..., :half]
    second = field[..., half:]
    return jnp.concatenate(
        [first * cosine - second * sine, second * cosine + first * sine], axis=-1
    )


def local(tokens, norm_gain, wq, wk, wv, wo, doc_ids):
    tok_rows = tokens.shape[0]
    head_size = HEAD_WIDTH
    kv_local = wk.shape[1] // head_size
    query_group = QUERY_HEADS // KV_HEAD_COUNT
    source = tokens.astype(jnp.float32)
    whole = lax.all_gather(tokens, "head", axis=1, tiled=True).astype(jnp.float32)
    mean_sq = jnp.mean(whole * whole, axis=1, keepdims=True)
    normed_input = (whole * lax.rsqrt(mean_sq + 1e-05) * norm_gain[None, :]).astype(jnp.bfloat16)
    query_acc = jnp.dot(
        normed_input,
        lax.all_gather(wq, ("seq", "srv"), axis=0, tiled=True),
        preferred_element_type=jnp.float32,
    )
    key_acc = jnp.dot(
        normed_input,
        lax.all_gather(wk, ("seq", "srv"), axis=0, tiled=True),
        preferred_element_type=jnp.float32,
    )
    value_acc = jnp.dot(
        normed_input,
        lax.all_gather(wv, ("seq", "srv"), axis=0, tiled=True),
        preferred_element_type=jnp.float32,
    )
    first_pos = lax.axis_index(("seq", "srv")) * tok_rows
    positions = first_pos + jnp.arange(tok_rows, dtype=jnp.int32)
    query_matrix = rope(query_acc.reshape(tok_rows, kv_local * query_group, head_size), positions)
    query_matrix = query_matrix.astype(jnp.bfloat16).reshape(
        tok_rows, kv_local, query_group, head_size
    )
    key_matrix = rope(key_acc.reshape(tok_rows, kv_local, head_size), positions).astype(
        jnp.bfloat16
    )
    key_matrix = key_matrix.reshape(tok_rows, kv_local * head_size)
    value_matrix = value_acc.astype(jnp.bfloat16)
    scale = 1.0 / head_size**0.5

    def attend_block(carry, key_rows, value_rows, doc_rows, key_pos):
        run_top, run_total, run_acc = carry
        key_heads = key_rows.reshape(key_rows.shape[0], kv_local, head_size)
        value_heads = value_rows.reshape(value_rows.shape[0], kv_local, head_size)
        scores = (
            jnp.einsum(
                "qcgd,kcd->qcgk", query_matrix, key_heads, preferred_element_type=jnp.float32
            )
            * scale
        )
        allowed = (
            (key_pos[None, :] <= positions[:, None])
            & (key_pos[None, :] >= 0)
            & (doc_rows[None, :] == doc_ids[:, None])
        )
        allowed = allowed[:, None, None, :]
        masked = jnp.where(allowed, scores, -1e30)
        new_top = jnp.maximum(run_top, jnp.max(masked, axis=3))
        expd = jnp.where(allowed, jnp.exp(masked - new_top[..., None]), 0.0)
        factor = jnp.exp(run_top - new_top)
        new_total = run_total * factor + jnp.sum(expd, axis=3)
        weights = expd.astype(jnp.bfloat16)
        update = jnp.einsum(
            "qcgk,kcd->qcgd", weights, value_heads, preferred_element_type=jnp.float32
        )
        return (new_top, new_total, run_acc * factor[..., None] + update)

    start_state = (
        jnp.full((tok_rows, kv_local, query_group), -1e30, jnp.float32),
        jnp.zeros((tok_rows, kv_local, query_group), jnp.float32),
        jnp.zeros((tok_rows, kv_local, query_group, head_size), jnp.float32),
    )
    key_piece = lax.all_gather(key_matrix, ("seq", "srv"), axis=0, tiled=True)
    value_piece = lax.all_gather(value_matrix, ("seq", "srv"), axis=0, tiled=True)
    doc_piece = lax.all_gather(doc_ids, ("seq", "srv"), axis=0, tiled=True)
    count = key_piece.shape[0]
    width = math.gcd(count, 512)

    def step(inner, index):
        offset = index * width
        key_rows = lax.dynamic_slice_in_dim(key_piece, offset, width, 0)
        value_rows = lax.dynamic_slice_in_dim(value_piece, offset, width, 0)
        doc_rows = lax.dynamic_slice_in_dim(doc_piece, offset, width, 0)
        key_pos = offset + jnp.arange(width, dtype=jnp.int32)
        return (attend_block(inner, key_rows, value_rows, doc_rows, key_pos), None)

    def run_all(inner):
        result, _ = lax.scan(step, inner, jnp.arange(count // width, dtype=jnp.int32))
        return result

    beyond = jnp.int32(0) > first_pos + tok_rows - 1
    before = doc_piece[count - 1] < doc_ids[0]
    _, final_total, final_acc = lax.cond(beyond | before, lambda inner: inner, run_all, start_state)
    attended = (final_acc / final_total[..., None]).astype(jnp.bfloat16)
    attended = attended.reshape(tok_rows, kv_local * query_group * head_size)
    terms = jnp.dot(
        attended,
        lax.all_gather(wo, ("seq", "srv"), axis=1, tiled=True),
        preferred_element_type=jnp.float32,
    )
    summed = lax.psum_scatter(
        terms.astype(jnp.bfloat16), "head", scatter_dimension=1, tiled=True
    ).astype(jnp.float32)
    return (source + summed).astype(jnp.bfloat16)


def solution(mesh):
    sizes = dict(mesh.shape)
    if sizes["grp"] == 1 and sizes["head"] == 1 and sizes["seq"] == 16 and sizes["srv"] == 2:
        fine = Mesh(np.asarray(mesh.devices).reshape(2, 2, 2, 2, 2), AXES)
        in_specs = (P(AXES), P(), P(AXES), P(AXES), P(AXES), P(None, AXES), P(AXES))
        return jax.shard_map(
            split_body, mesh=fine, in_specs=in_specs, out_specs=P(AXES), check_vma=False
        )
    in_specs = (
        P(("grp", "seq", "srv"), "head"),
        P(),
        P(("seq", "srv"), "head"),
        P(("seq", "srv"), "head"),
        P(("seq", "srv"), "head"),
        P("head", ("seq", "srv")),
        P(("grp", "seq", "srv")),
    )
    out_specs = P(("grp", "seq", "srv"), "head")
    return jax.shard_map(local, mesh=mesh, in_specs=in_specs, out_specs=out_specs, check_vma=False)
```

```python
import functools
import math

import jax
import jax.numpy as jnp
import numpy as np
from jax import lax
from jax.experimental import pallas as pl
from jax.experimental.pallas import tpu as pltpu
from jax.sharding import Mesh
from jax.sharding import PartitionSpec as P

QUERY_HEADS = 32
KV_HEAD_COUNT = 8
HEAD_WIDTH = 128
DOCS = 8


AXES = ("zh", "zl", "y", "x", "c")
QUAD = ("zl", "x", "c")
SWAP = [(0, 1), (1, 0)]
EXTRA = 16
QT = 256
KT = 512
NEG = -1e30

ANY = pl.BlockSpec(memory_space=pl.ANY)
VMEM = pl.BlockSpec(memory_space=pltpu.VMEM)
SMEM = pl.BlockSpec(memory_space=pltpu.SMEM)


def swap(value, axis):
    return lax.ppermute(value, axis, SWAP)


def quad_gather(block, by_z_first):
    by_x = swap(block, "x")
    by_z = swap(block, "zl")
    far = swap(by_z, "x") if by_z_first else swap(by_x, "zl")
    got = {(0, 0): block, (0, 1): by_x, (1, 0): by_z, (1, 1): far}
    out = {}
    for (dzl, dx), piece in got.items():
        out[dzl, dx, 0] = piece
        out[dzl, dx, 1] = swap(piece, "c")
    return out


OFFSETS = [(dzl, dx, dc) for dzl in range(2) for dx in range(2) for dc in range(2)]


def start_copies(copies, sems, first=0):
    started = []
    for i, (src, dst) in enumerate(copies):
        copy = pltpu.make_async_copy(src, dst, sems.at[first + i])
        copy.start()
        started.append(copy)
    return started


def wait_all(copies):
    for copy in copies:
        copy.wait()


def aligned(value, step):
    return pl.multiple_of(value, step)


def layout_kernel(wk_ref, wv_ref, doc_ref, out_ref):
    for j in range(8):
        out_ref[j, :128, :128] = wk_ref[:, 128 * j : 128 * j + 128]
        out_ref[j, :128, 128:] = wv_ref[:, 128 * j : 128 * j + 128]
    below = doc_ref[...] < lax.broadcasted_iota(jnp.int32, (EXTRA, 128), 0)
    count = jnp.sum(jnp.where(below, 1.0, 0.0), axis=1, keepdims=True)
    rows = jnp.broadcast_to(count, (EXTRA, 256)).astype(jnp.bfloat16)
    for j in range(8):
        out_ref[j, 128:, :] = rows


TOKEN_PIECES = [
    (dzl, dx, dc, first, rows)
    for dzl, dx, first, rows in (
        (0, 0, 0, 128),
        (0, 1, 0, 128),
        (1, 0, 0, 64),
        (1, 0, 64, 64),
        (1, 1, 0, 64),
        (1, 1, 64, 64),
    )
    for dc in range(2)
]


def token_copies(dzl, where, tok_refs, xs):
    zl, x, c = where[1], where[3], where[4]
    copies = []
    for (piece_dzl, dx, dc, first, rows), ref in zip(TOKEN_PIECES, tok_refs):
        if piece_dzl == dzl:
            slot = 4 * (zl ^ dzl) + 2 * (x ^ dx) + (c ^ dc)
            copies.append((ref, xs.at[pl.ds(aligned(slot * 128 + first, 64), rows), :]))
    return copies


def weight_row(where, dzh, dy, zlp):
    return aligned((4 * (where[0] ^ dzh) + 2 * zlp + (where[2] ^ dy)) * 512, 512)


def turn(part, cos_ref, sin_ref, rows):
    return part * cos_ref[rows, :] + pltpu.roll(part, 64, axis=1) * sin_ref[rows, :]


def project_kv_kernel(where, *refs):
    tok_refs, wkv_refs, (cos_ref, sin_ref) = refs[:12], refs[12:16], refs[16:18]
    kv_out, xs, wkv, sems = refs[18:]
    copies = []
    for (dzh, dy), ref in zip(((0, 0), (0, 1), (1, 0), (1, 1)), wkv_refs):
        for j in range(8):
            row = aligned(weight_row(where, dzh, dy, j // 4) + (j % 4) * 128, 128)
            copies.append((ref.at[j, pl.ds(0, 128), :], wkv.at[pl.ds(row, 128), :]))
    near = start_copies(token_copies(0, where, tok_refs, xs), sems)
    near += start_copies(copies, sems, 4)
    far = start_copies(token_copies(1, where, tok_refs, xs), sems, 36)
    for dzl, waits in enumerate((near, far)):
        wait_all(waits)
        rows = pl.ds(aligned((where[1] ^ dzl) * 512, 512), 512)
        acc = jnp.dot(xs[rows, :], wkv[...], preferred_element_type=jnp.float32)
        kv_out[rows, :128] = turn(acc[:, :128], cos_ref, sin_ref, rows).astype(jnp.bfloat16)
        kv_out[rows, 128:] = acc[:, 128:].astype(jnp.bfloat16)


def project_q_kernel(where, *refs):
    tok_refs = refs[:12]
    wq_own, wq_y, wq_z0, wq_z1, wq_zy0, wq_zy1, cos_ref, sin_ref = refs[12:20]
    q_out, xs, wq, sems = refs[20:]
    copies = []
    for zlp in range(2):
        for dzh, dy, src in (
            (0, 0, wq_own.at[pl.ds(zlp * 512, 512), :]),
            (0, 1, wq_y.at[pl.ds(zlp * 512, 512), :]),
            (1, 0, (wq_z0, wq_z1)[zlp]),
            (1, 1, (wq_zy0, wq_zy1)[zlp]),
        ):
            copies.append((src, wq.at[pl.ds(weight_row(where, dzh, dy, zlp), 512), :]))
    near = start_copies(token_copies(0, where, tok_refs, xs), sems)
    near += start_copies(copies, sems, 4)
    far = start_copies(token_copies(1, where, tok_refs, xs), sems, 12)
    for dzl, waits in enumerate((near, far)):
        wait_all(waits)
        rows = pl.ds(aligned((where[1] ^ dzl) * 512, 512), 512)
        for n in range(2):
            acc = jnp.dot(
                xs[rows, :], wq[:, 256 * n : 256 * n + 256], preferred_element_type=jnp.float32
            )
            for k in range(2):
                part = turn(acc[:, 128 * k : 128 * k + 128], cos_ref, sin_ref, rows)
                columns = slice(256 * n + 128 * k, 256 * n + 128 * k + 128)
                q_out[rows, columns] = part.astype(jnp.bfloat16)


FACTOR = math.log2(math.e) / math.sqrt(HEAD_WIDTH)


def first_position(zh, y, tile):
    return (2 * zh + tile // 2) * 1024 + y * 512 + (tile % 2) * QT


def copy_keys(kv_refs, y, ks, vs, sems):
    copies = []
    for dy, ref in enumerate(kv_refs):
        for zlp in range(2):
            row = aligned((2 * zlp + (y ^ dy)) * 512, 512)
            for half, dst in ((0, ks), (1, vs)):
                src = ref.at[pl.ds(zlp * 512, 512), pl.ds(half * 128, 128)]
                copies.append((src, dst.at[pl.ds(row, 512), :]))
    wait_all(start_copies(copies, sems))


def attend_step(queries, keys, values, state, mask):
    top, total, acc = state
    scores = lax.dot_general(
        queries, keys, (((1,), (1,)), ((), ())), preferred_element_type=jnp.float32
    )
    if mask is not None:
        scores = jnp.where(mask[None], scores.reshape(4, QT, KT), NEG).reshape(4 * QT, KT)
    cuts = [slice(128 * i, 128 * i + 128) for i in range(KT // 128)]
    best = functools.reduce(jnp.maximum, [scores[:, cut] for cut in cuts])
    old = top[...]
    new = jnp.maximum(old, jnp.max(best, axis=1, keepdims=True))
    top[...] = new
    shrink = jnp.exp2((old - new) * FACTOR)
    parts = [jnp.exp2((scores[:, cut] - new) * FACTOR) for cut in cuts]
    total[...] = total[...] * shrink + functools.reduce(jnp.add, parts)
    weights = jnp.concatenate([part.astype(jnp.bfloat16) for part in parts], axis=1)
    acc[...] = acc[...] * shrink + jnp.dot(weights, values, preferred_element_type=jnp.float32)


def stacked(q_ref):
    return jnp.concatenate([q_ref[:, 128 * h : 128 * h + 128] for h in range(4)], axis=0)


def near_kernel(half, where, tile_lo, tile_hi, q_ref, start_ref, kv_own, kv_y, *refs):
    top, total, acc, ks, vs, sems = refs
    zh, y = where[0], where[2]
    tile = 2 * half + pl.program_id(0)

    @pl.when(pl.program_id(0) == 0)
    def _():
        copy_keys((kv_own, kv_y), y, ks, vs, sems)

    state = (top.at[0], total.at[0], acc.at[0])
    state[0][...] = jnp.full((4 * QT, 128), NEG, jnp.float32)
    state[1][...] = jnp.zeros((4 * QT, 128), jnp.float32)
    state[2][...] = jnp.zeros((4 * QT, 128), jnp.float32)
    first = first_position(zh, y, tile)
    base = zh * (2048 // KT)

    @pl.loop(jnp.maximum(tile_lo[tile] // KT, base), (first + QT + KT - 1) // KT)
    def _(block):
        keys = pl.ds(aligned((block - base) * KT, KT), KT)
        edge = (block * KT + KT - 1 > first) | (block * KT < tile_hi[tile])

        @pl.when(edge)
        def _():
            key_pos = block * KT + lax.broadcasted_iota(jnp.int32, (QT, KT), 1)
            query_pos = first + lax.broadcasted_iota(jnp.int32, (QT, KT), 0)
            mask = (key_pos <= query_pos) & (key_pos >= start_ref[:, :1])
            attend_step(stacked(q_ref), ks[keys, :], vs[keys, :], state, mask)

        @pl.when(jnp.logical_not(edge))
        def _():
            attend_step(stacked(q_ref), ks[keys, :], vs[keys, :], state, None)


def far_kernel(half, where, tile_lo, tile_hi, q_ref, start_ref, kv_z, kv_zy, *refs):
    top_in, total_in, acc_in, out_ref, ks, vs, top, total, acc, sems = refs
    zh, y = where[0], where[2]
    tile = 2 * half + pl.program_id(0)

    @pl.when((pl.program_id(0) == 0) & (zh == 1))
    def _():
        copy_keys((kv_z, kv_zy), y, ks, vs, sems)

    top[...] = top_in[0]
    total[...] = total_in[0]
    acc[...] = acc_in[0]

    @pl.loop(tile_lo[tile] // KT, zh * (2048 // KT))
    def _(block):
        keys = pl.ds(aligned(block * KT, KT), KT)
        edge = block * KT < tile_hi[tile]

        @pl.when(edge)
        def _():
            key_pos = block * KT + lax.broadcasted_iota(jnp.int32, (QT, KT), 1)
            mask = key_pos >= start_ref[:, :1]
            attend_step(stacked(q_ref), ks[keys, :], vs[keys, :], (top, total, acc), mask)

        @pl.when(jnp.logical_not(edge))
        def _():
            attend_step(stacked(q_ref), ks[keys, :], vs[keys, :], (top, total, acc), None)

    result = acc[...] / jnp.sum(total[...], axis=1, keepdims=True)
    for h in range(4):
        out_ref[:, 128 * h : 128 * h + 128] = result[QT * h : QT * h + QT].astype(jnp.bfloat16)


def output_kernel(with_first, where, *refs):
    att_refs = refs[:8]
    wo_refs = refs[8:16]
    rest = refs[16:]
    out_ref, xs, wo, sems = rest[-4:]
    zh, zl, y, x, c = (where[i] for i in range(5))
    copies = []
    for (dzl, dx, dc), ref in zip(OFFSETS, att_refs):
        slot = 4 * (zl ^ dzl) + 2 * (x ^ dx) + (c ^ dc)
        copies.append((ref, xs.at[:, pl.ds(aligned(slot * 512, 512), 512)]))
    for i, ref in enumerate(wo_refs):
        column = aligned((2 * (zh ^ (i // 2 % 2)) + (y ^ (i % 2))) * 128, 128)
        copies.append((ref, wo.at[2048 * (i // 4) : 2048 * (i // 4) + 2048, pl.ds(column, 128)]))
    started = start_copies(copies, sems)
    base = 0
    if with_first:
        base = 512
        out_ref[:512, :] = rest[0][...]
    wait_all(started)
    for n in range(2):
        columns = slice(256 * n, 256 * n + 256)
        acc = jnp.dot(xs[...], wo[:, columns], preferred_element_type=jnp.float32)
        out_ref[base : base + 512, columns] = acc.astype(jnp.bfloat16)


def finish_kernel(tok_ref, sent_ref, out_ref):
    for block in range(32):
        zhp, zlp, yp, xp, cp = ((block >> s) & 1 for s in (4, 3, 2, 1, 0))
        source, part = 4 * zlp + 2 * xp + cp, 2 * zhp + yp
        columns = slice(128 * block, 128 * block + 128)
        sent = sent_ref[source, :, 128 * part : 128 * part + 128].astype(jnp.float32)
        out_ref[:, columns] = (tok_ref[:, columns].astype(jnp.float32) + sent).astype(jnp.bfloat16)


def call(kernel, out_shape, in_specs, scratch, cost, **more):
    flops, moved = cost
    more.setdefault("out_specs", jax.tree.map(lambda _: VMEM, out_shape))
    return pl.pallas_call(
        kernel,
        out_shape=out_shape,
        in_specs=in_specs,
        scratch_shapes=scratch,
        compiler_params=pltpu.CompilerParams(vmem_limit_bytes=48 * 1024 * 1024),
        cost_estimate=pl.CostEstimate(flops=flops, bytes_accessed=moved, transcendentals=0),
        **more,
    )


def split_body(tokens, norm_gain, wq, wk, wv, wo, doc_ids):
    bf16, f32 = jnp.bfloat16, jnp.float32
    zh, zl, y, x, c = place = [lax.axis_index(axis) for axis in AXES]
    where = jnp.stack(place).astype(jnp.int32)

    wkv = call(
        layout_kernel,
        jax.ShapeDtypeStruct((8, 128 + EXTRA, 256), bf16),
        [VMEM] * 3,
        [],
        (128 * EXTRA, 1 << 20),
    )(wk, wv, doc_ids.reshape(1, 128))
    wkv = lax.all_to_all(wkv, QUAD, 0, 0, tiled=True)
    wkv_z = swap(wkv, "zh")
    wkvs = [wkv, swap(wkv, "y"), wkv_z, swap(wkv_z, "y")]

    wqs = jnp.transpose(wq.reshape(128, 8, 512), (1, 0, 2))
    wqs = lax.all_to_all(wqs, QUAD, 0, 0, tiled=True).reshape(1024, 512)
    wq_z0 = swap(wqs[:512], "zh")
    wq_z1 = swap(wqs[512:], "zh")
    wq_y = swap(wqs, "y")
    wq_zy0 = swap(wq_z0, "y")
    wq_zy1 = swap(wq_z1, "y")

    source = tokens.astype(f32)
    mean_sq = jnp.mean(source * source, axis=1, keepdims=True)
    normed = (source * lax.rsqrt(mean_sq + 1e-05) * norm_gain[None, :]).astype(bf16)
    tok_z = [swap(normed[64 * i : 64 * i + 64], "zl") for i in range(2)]
    tok_far = [swap(tok_z[i], "x") for i in range(2)]
    tok = []
    for piece in [normed, swap(normed, "x"), *tok_z, *tok_far]:
        tok += [piece, swap(piece, "c")]

    token = jnp.arange(1024, dtype=jnp.int32)
    positions = (2 * zh + token // 512) * 1024 + y * 512 + token % 512
    freqs = 500000.0 ** (-(jnp.arange(64, dtype=f32) * 2.0 / HEAD_WIDTH))
    angles = positions.astype(f32)[:, None] * freqs[None, :]
    cosine, sine = jnp.cos(angles), jnp.sin(angles)
    cosine = jnp.concatenate([cosine, cosine], axis=1)
    sine = jnp.concatenate([-sine, sine], axis=1)

    counts = jnp.concatenate([piece[:, 128 : 128 + DOCS, 0] for piece in wkvs], axis=0)
    starts = jnp.sum(counts.astype(f32), axis=0).astype(jnp.int32)
    query_start = jnp.max(
        jnp.where(positions[:, None] >= starts[None, :], starts[None, :], 0), axis=1
    )
    tile_lo = query_start[::QT]
    tile_hi = query_start[QT - 1 :: QT]
    start_col = jnp.broadcast_to(query_start[:, None], (1024, 128))

    keys_values = call(
        project_kv_kernel,
        jax.ShapeDtypeStruct((1024, 256), bf16),
        [SMEM] + [ANY] * 16 + [VMEM, VMEM],
        [
            pltpu.VMEM((1024, 4096), bf16),
            pltpu.VMEM((4096, 256), bf16),
            pltpu.SemaphoreType.DMA((44,)),
        ],
        (2 * 1024 * 4096 * 256, 11 << 20),
    )(where, *tok, *wkvs, cosine, sine)
    queries = call(
        project_q_kernel,
        jax.ShapeDtypeStruct((1024, 512), bf16),
        [SMEM] + [ANY] * 18 + [VMEM, VMEM],
        [
            pltpu.VMEM((1024, 4096), bf16),
            pltpu.VMEM((4096, 512), bf16),
            pltpu.SemaphoreType.DMA((20,)),
        ],
        (2 * 1024 * 4096 * 512, 14 << 20),
    )(where, *tok, wqs, wq_y, wq_z0, wq_z1, wq_zy0, wq_zy1, cosine, sine)

    kv_y = swap(keys_values, "y")
    kv_z = swap(keys_values, "zh")
    kv_zy = swap(kv_z, "y")

    def tile_spec(shape, first):
        return pl.BlockSpec(shape, lambda i: (i + first,) + (0,) * (len(shape) - 1))

    def state_specs():
        return [tile_spec((1, 4 * QT, 128), 0)] * 3

    def near_half(half):
        return call(
            functools.partial(near_kernel, half),
            [jax.ShapeDtypeStruct((2, 4 * QT, 128), f32)] * 3,
            [SMEM] * 3
            + [tile_spec((QT, 512), 2 * half), tile_spec((QT, 128), 2 * half), ANY, ANY],
            [
                pltpu.VMEM((2048, 128), bf16),
                pltpu.VMEM((2048, 128), bf16),
                pltpu.SemaphoreType.DMA((8,)),
            ],
            (4 * 512 * 2048 * 512, 4 << 20),
            grid=(2,),
            out_specs=state_specs(),
        )(where, tile_lo, tile_hi, queries, start_col, keys_values, kv_y)

    state = [near_half(0), near_half(1)]

    def far_call(half):
        return call(
            functools.partial(far_kernel, half),
            jax.ShapeDtypeStruct((512, 512), bf16),
            [SMEM, SMEM, SMEM, tile_spec((QT, 512), 2 * half), tile_spec((QT, 128), 2 * half)]
            + [ANY, ANY] + state_specs(),
            [
                pltpu.VMEM((2048, 128), bf16),
                pltpu.VMEM((2048, 128), bf16),
                pltpu.VMEM((4 * QT, 128), f32),
                pltpu.VMEM((4 * QT, 128), f32),
                pltpu.VMEM((4 * QT, 128), f32),
                pltpu.SemaphoreType.DMA((8,)),
            ],
            (4 * 512 * 2048 * 512, 8 << 20),
            grid=(2,),
            out_specs=pl.BlockSpec((QT, 512), lambda i: (i, 0)),
        )(where, tile_lo, tile_hi, queries, start_col, kv_z, kv_zy, *state[half])

    attended = [far_call(0), far_call(1)]

    wos = []
    for part in range(2):
        piece = wo[2048 * part : 2048 * part + 2048]
        by_z = swap(piece, "zh")
        wos += [piece, swap(piece, "y"), by_z, swap(by_z, "y")]

    def output(half, first):
        att = quad_gather(attended[half], half == 1)
        rows = 1024 if first else 512
        return output_call(att, first, rows)

    def output_call(att, first, rows):
        return call(
            functools.partial(output_kernel, bool(first)),
            jax.ShapeDtypeStruct((rows, 512), bf16),
            [SMEM] + [ANY] * 16 + [VMEM] * len(first),
            [
                pltpu.VMEM((512, 4096), bf16),
                pltpu.VMEM((4096, 512), bf16),
                pltpu.SemaphoreType.DMA((16,)),
            ],
            (2 * 512 * 4096 * 512, 9 << 20),
        )(where, *[att[at] for at in OFFSETS], *wos, *first)

    sent = output(1, [output(0, [])])
    home = lax.all_to_all(sent.reshape(8, 128, 512), QUAD, 0, 0, tiled=True)
    return call(
        finish_kernel,
        jax.ShapeDtypeStruct((128, 4096), bf16),
        [VMEM, VMEM],
        [],
        (128 * 4096, 3 << 20),
    )(tokens, home)


def rope(field, positions):
    half = field.shape[-1] // 2
    freqs = 500000.0 ** (-(jnp.arange(half, dtype=jnp.float32) * 2.0 / field.shape[-1]))
    angles = positions.astype(jnp.float32)[:, None] * freqs[None, :]
    cosine = jnp.cos(angles)[:, None, :]
    sine = jnp.sin(angles)[:, None, :]
    first = field[..., :half]
    second = field[..., half:]
    return jnp.concatenate(
        [first * cosine - second * sine, second * cosine + first * sine], axis=-1
    )


def local(tokens, norm_gain, wq, wk, wv, wo, doc_ids):
    tok_rows = tokens.shape[0]
    head_size = HEAD_WIDTH
    kv_local = wk.shape[1] // head_size
    query_group = QUERY_HEADS // KV_HEAD_COUNT
    source = tokens.astype(jnp.float32)
    whole = lax.all_gather(tokens, "head", axis=1, tiled=True).astype(jnp.float32)
    mean_sq = jnp.mean(whole * whole, axis=1, keepdims=True)
    normed_input = (whole * lax.rsqrt(mean_sq + 1e-05) * norm_gain[None, :]).astype(jnp.bfloat16)
    query_acc = jnp.dot(
        normed_input,
        lax.all_gather(wq, ("seq", "srv"), axis=0, tiled=True),
        preferred_element_type=jnp.float32,
    )
    key_acc = jnp.dot(
        normed_input,
        lax.all_gather(wk, ("seq", "srv"), axis=0, tiled=True),
        preferred_element_type=jnp.float32,
    )
    value_acc = jnp.dot(
        normed_input,
        lax.all_gather(wv, ("seq", "srv"), axis=0, tiled=True),
        preferred_element_type=jnp.float32,
    )
    first_pos = lax.axis_index(("seq", "srv")) * tok_rows
    positions = first_pos + jnp.arange(tok_rows, dtype=jnp.int32)
    query_matrix = rope(query_acc.reshape(tok_rows, kv_local * query_group, head_size), positions)
    query_matrix = query_matrix.astype(jnp.bfloat16).reshape(
        tok_rows, kv_local, query_group, head_size
    )
    key_matrix = rope(key_acc.reshape(tok_rows, kv_local, head_size), positions).astype(
        jnp.bfloat16
    )
    key_matrix = key_matrix.reshape(tok_rows, kv_local * head_size)
    value_matrix = value_acc.astype(jnp.bfloat16)
    scale = 1.0 / head_size**0.5

    def attend_block(carry, key_rows, value_rows, doc_rows, key_pos):
        run_top, run_total, run_acc = carry
        key_heads = key_rows.reshape(key_rows.shape[0], kv_local, head_size)
        value_heads = value_rows.reshape(value_rows.shape[0], kv_local, head_size)
        scores = (
            jnp.einsum(
                "qcgd,kcd->qcgk", query_matrix, key_heads, preferred_element_type=jnp.float32
            )
            * scale
        )
        allowed = (
            (key_pos[None, :] <= positions[:, None])
            & (key_pos[None, :] >= 0)
            & (doc_rows[None, :] == doc_ids[:, None])
        )
        allowed = allowed[:, None, None, :]
        masked = jnp.where(allowed, scores, -1e30)
        new_top = jnp.maximum(run_top, jnp.max(masked, axis=3))
        expd = jnp.where(allowed, jnp.exp(masked - new_top[..., None]), 0.0)
        factor = jnp.exp(run_top - new_top)
        new_total = run_total * factor + jnp.sum(expd, axis=3)
        weights = expd.astype(jnp.bfloat16)
        update = jnp.einsum(
            "qcgk,kcd->qcgd", weights, value_heads, preferred_element_type=jnp.float32
        )
        return (new_top, new_total, run_acc * factor[..., None] + update)

    start_state = (
        jnp.full((tok_rows, kv_local, query_group), -1e30, jnp.float32),
        jnp.zeros((tok_rows, kv_local, query_group), jnp.float32),
        jnp.zeros((tok_rows, kv_local, query_group, head_size), jnp.float32),
    )
    key_piece = lax.all_gather(key_matrix, ("seq", "srv"), axis=0, tiled=True)
    value_piece = lax.all_gather(value_matrix, ("seq", "srv"), axis=0, tiled=True)
    doc_piece = lax.all_gather(doc_ids, ("seq", "srv"), axis=0, tiled=True)
    count = key_piece.shape[0]
    width = math.gcd(count, 512)

    def step(inner, index):
        offset = index * width
        key_rows = lax.dynamic_slice_in_dim(key_piece, offset, width, 0)
        value_rows = lax.dynamic_slice_in_dim(value_piece, offset, width, 0)
        doc_rows = lax.dynamic_slice_in_dim(doc_piece, offset, width, 0)
        key_pos = offset + jnp.arange(width, dtype=jnp.int32)
        return (attend_block(inner, key_rows, value_rows, doc_rows, key_pos), None)

    def run_all(inner):
        result, _ = lax.scan(step, inner, jnp.arange(count // width, dtype=jnp.int32))
        return result

    beyond = jnp.int32(0) > first_pos + tok_rows - 1
    before = doc_piece[count - 1] < doc_ids[0]
    _, final_total, final_acc = lax.cond(beyond | before, lambda inner: inner, run_all, start_state)
    attended = (final_acc / final_total[..., None]).astype(jnp.bfloat16)
    attended = attended.reshape(tok_rows, kv_local * query_group * head_size)
    terms = jnp.dot(
        attended,
        lax.all_gather(wo, ("seq", "srv"), axis=1, tiled=True),
        preferred_element_type=jnp.float32,
    )
    summed = lax.psum_scatter(
        terms.astype(jnp.bfloat16), "head", scatter_dimension=1, tiled=True
    ).astype(jnp.float32)
    return (source + summed).astype(jnp.bfloat16)


def solution(mesh):
    sizes = dict(mesh.shape)
    if sizes["grp"] == 1 and sizes["head"] == 1 and sizes["seq"] == 16 and sizes["srv"] == 2:
        fine = Mesh(np.asarray(mesh.devices).reshape(2, 2, 2, 2, 2), AXES)
        in_specs = (P(AXES), P(), P(AXES), P(AXES), P(AXES), P(None, AXES), P(AXES))
        return jax.shard_map(
            split_body, mesh=fine, in_specs=in_specs, out_specs=P(AXES), check_vma=False
        )
    in_specs = (
        P(("grp", "seq", "srv"), "head"),
        P(),
        P(("seq", "srv"), "head"),
        P(("seq", "srv"), "head"),
        P(("seq", "srv"), "head"),
        P("head", ("seq", "srv")),
        P(("grp", "seq", "srv")),
    )
    out_specs = P(("grp", "seq", "srv"), "head")
    return jax.shard_map(local, mesh=mesh, in_specs=in_specs, out_specs=out_specs, check_vma=False)
```

```python
import functools
import math

import jax
import jax.numpy as jnp
import numpy as np
from jax import lax
from jax.experimental import pallas as pl
from jax.experimental.pallas import tpu as pltpu
from jax.sharding import Mesh
from jax.sharding import PartitionSpec as P

QUERY_HEADS = 32
KV_HEAD_COUNT = 8
HEAD_WIDTH = 128
DOCS = 8


AXES = ("zh", "zl", "y", "x", "c")
QUAD = ("zl", "x", "c")
SWAP = [(0, 1), (1, 0)]
EXTRA = 8
QT = 256
KT = 512
NEG = -1e30

ANY = pl.BlockSpec(memory_space=pl.ANY)
VMEM = pl.BlockSpec(memory_space=pltpu.VMEM)
SMEM = pl.BlockSpec(memory_space=pltpu.SMEM)


def swap(value, axis):
    return lax.ppermute(value, axis, SWAP)


def quad_gather(block, by_z_first):
    by_x = swap(block, "x")
    by_z = swap(block, "zl")
    far = swap(by_z, "x") if by_z_first else swap(by_x, "zl")
    got = {(0, 0): block, (0, 1): by_x, (1, 0): by_z, (1, 1): far}
    out = {}
    for (dzl, dx), piece in got.items():
        out[dzl, dx, 0] = piece
        out[dzl, dx, 1] = swap(piece, "c")
    return out


OFFSETS = [(dzl, dx, dc) for dzl in range(2) for dx in range(2) for dc in range(2)]


def start_copies(copies, sems, first=0):
    started = []
    for i, (src, dst) in enumerate(copies):
        copy = pltpu.make_async_copy(src, dst, sems.at[first + i])
        copy.start()
        started.append(copy)
    return started


def wait_all(copies):
    for copy in copies:
        copy.wait()


def aligned(value, step):
    return pl.multiple_of(value, step)


def layout_kernel(wq_ref, wk_ref, wv_ref, doc_ref, out_ref):
    below = doc_ref[...] < lax.broadcasted_iota(jnp.int32, (EXTRA, 128), 0)
    count = jnp.sum(jnp.where(below, 1.0, 0.0), axis=1, keepdims=True)
    rows = jnp.broadcast_to(count, (EXTRA, 768)).astype(jnp.bfloat16)
    for j in range(8):
        out_ref[j, :128, :512] = wq_ref[:, 512 * j : 512 * j + 512]
        out_ref[j, :128, 512:640] = wk_ref[:, 128 * j : 128 * j + 128]
        out_ref[j, :128, 640:] = wv_ref[:, 128 * j : 128 * j + 128]
        out_ref[j, 128:, :] = rows


TOKEN_PIECES = [
    (dzl, dx, dc, first, rows)
    for dzl, dx, first, rows in (
        (0, 0, 0, 128),
        (0, 1, 0, 128),
        (1, 0, 0, 64),
        (1, 0, 64, 64),
        (1, 1, 0, 64),
        (1, 1, 64, 64),
    )
    for dc in range(2)
]


def token_copies(dzl, where, tok_refs, xs):
    zl, x, c = where[1], where[3], where[4]
    copies = []
    for (piece_dzl, dx, dc, first, rows), ref in zip(TOKEN_PIECES, tok_refs):
        if piece_dzl == dzl:
            slot = 4 * (zl ^ dzl) + 2 * (x ^ dx) + (c ^ dc)
            copies.append((ref, xs.at[pl.ds(aligned(slot * 128 + first, 64), rows), :]))
    return copies


def weight_copies(where, pieces, dst):
    copies = []
    for dzh, dy, ref, source, target in pieces:
        for zlp in range(2):
            block = 4 * (where[0] ^ dzh) + 2 * zlp + (where[2] ^ dy)
            src = ref.at[pl.ds(4 * zlp, 4), pl.ds(0, 128), source]
            copies.append((src, dst.at[pl.ds(4 * block, 4), :, target]))
    return copies


def turn(part, cos_ref, sin_ref, rows):
    return part * cos_ref[rows, :] + pltpu.roll(part, 64, axis=1) * sin_ref[rows, :]


def project_kv_kernel(where, count_ref, *refs):
    tok_refs, (w_own, w_y, w_z, w_zy, cos_ref, sin_ref) = refs[:12], refs[12:18]
    kv_out, start_out, bounds_out, xs, wkv, sems = refs[18:]
    zh, zl, y = where[0], where[1], where[2]
    columns, whole = pl.ds(512, 256), pl.ds(0, 256)
    near = start_copies(token_copies(0, where, tok_refs, xs), sems)
    pieces = (
        (0, 0, w_own, columns, whole),
        (0, 1, w_y, columns, whole),
        (1, 0, w_z, whole, whole),
        (1, 1, w_zy, whole, whole),
    )
    near += start_copies(weight_copies(where, pieces, wkv), sems, 4)
    far = start_copies(token_copies(1, where, tok_refs, xs), sems, 12)

    counts = jnp.sum(count_ref[...].astype(jnp.float32), axis=0).astype(jnp.int32)
    for half in range(2):
        base = (2 * zh + half) * 1024 + y * 512
        position = base + lax.broadcasted_iota(jnp.int32, (512, 128), 0)
        start = jnp.zeros((512, 128), jnp.int32)
        for d in range(DOCS):
            row = counts[d : d + 1, :]
            start = jnp.maximum(start, jnp.where(position >= row, row, 0))
        start_out[512 * half : 512 * half + 512, :] = start
    document = [jnp.max(counts[d : d + 1, :]) for d in range(DOCS)]
    for tile in range(1024 // QT):
        first = first_position(zh, y, tile)
        for k, position in enumerate((first, first + QT - 1)):
            bound = jnp.int32(0)
            for d in range(DOCS):
                bound = jnp.maximum(bound, jnp.where(position >= document[d], document[d], 0))
            bounds_out[4 * k + tile] = bound

    for dzl, waits in enumerate((near, far)):
        wait_all(waits)
        rows = pl.ds(aligned((zl ^ dzl) * 512, 512), 512)
        weights = wkv[...].reshape(4096, 256)
        acc = jnp.dot(xs[rows, :], weights, preferred_element_type=jnp.float32)
        kv_out[rows, :128] = turn(acc[:, :128], cos_ref, sin_ref, rows).astype(jnp.bfloat16)
        kv_out[rows, 128:] = acc[:, 128:].astype(jnp.bfloat16)


def project_q_kernel(where, *refs):
    tok_refs = refs[:12]
    w_own, w_y, w_z0, w_z1, w_zy0, w_zy1, cos_ref, sin_ref = refs[12:20]
    q_out, xs, wq, sems = refs[20:]
    whole, left, right = pl.ds(0, 512), pl.ds(0, 256), pl.ds(256, 256)
    near = start_copies(token_copies(0, where, tok_refs, xs), sems)
    pieces = (
        (0, 0, w_own, whole, whole),
        (0, 1, w_y, whole, whole),
        (1, 0, w_z0, left, left),
        (1, 1, w_zy0, left, left),
        (1, 0, w_z1, left, right),
        (1, 1, w_zy1, left, right),
    )
    near += start_copies(weight_copies(where, pieces, wq), sems, 4)
    far = start_copies(token_copies(1, where, tok_refs, xs), sems, 16)
    for dzl, waits in enumerate((near, far)):
        wait_all(waits)
        rows = pl.ds(aligned((where[1] ^ dzl) * 512, 512), 512)
        for n in range(2):
            weights = wq[:, :, 256 * n : 256 * n + 256].reshape(4096, 256)
            acc = jnp.dot(xs[rows, :], weights, preferred_element_type=jnp.float32)
            for k in range(2):
                part = turn(acc[:, 128 * k : 128 * k + 128], cos_ref, sin_ref, rows)
                columns = slice(256 * n + 128 * k, 256 * n + 128 * k + 128)
                q_out[rows, columns] = part.astype(jnp.bfloat16)


FACTOR = math.log2(math.e) / math.sqrt(HEAD_WIDTH)


def first_position(zh, y, tile):
    return (2 * zh + tile // 2) * 1024 + y * 512 + (tile % 2) * QT


def copy_keys(kv_refs, y, ks, vs, sems):
    copies = []
    for dy, ref in enumerate(kv_refs):
        for zlp in range(2):
            row = aligned((2 * zlp + (y ^ dy)) * 512, 512)
            for half, dst in ((0, ks), (1, vs)):
                src = ref.at[pl.ds(zlp * 512, 512), pl.ds(half * 128, 128)]
                copies.append((src, dst.at[pl.ds(row, 512), :]))
    wait_all(start_copies(copies, sems))


def attend_step(queries, keys, values, state, mask):
    top, total, acc = state
    scores = lax.dot_general(
        queries, keys, (((1,), (1,)), ((), ())), preferred_element_type=jnp.float32
    )
    if mask is not None:
        scores = jnp.where(mask[None], scores.reshape(4, QT, KT), NEG).reshape(4 * QT, KT)
    cuts = [slice(128 * i, 128 * i + 128) for i in range(KT // 128)]
    best = functools.reduce(jnp.maximum, [scores[:, cut] for cut in cuts])
    old = top[...]
    new = jnp.maximum(old, jnp.max(best, axis=1, keepdims=True))
    top[...] = new
    shrink = jnp.exp2((old - new) * FACTOR)
    parts = [jnp.exp2((scores[:, cut] - new) * FACTOR) for cut in cuts]
    total[...] = total[...] * shrink + functools.reduce(jnp.add, parts)
    weights = jnp.concatenate([part.astype(jnp.bfloat16) for part in parts], axis=1)
    acc[...] = acc[...] * shrink + jnp.dot(weights, values, preferred_element_type=jnp.float32)


def stacked(q_ref):
    return jnp.concatenate([q_ref[:, 128 * h : 128 * h + 128] for h in range(4)], axis=0)


def near_kernel(half, where, bounds, q_ref, start_ref, kv_own, kv_y, *refs):
    top, total, acc, ks, vs, sems = refs
    zh, y = where[0], where[2]
    tile = 2 * half + pl.program_id(0)

    @pl.when(pl.program_id(0) == 0)
    def _():
        copy_keys((kv_own, kv_y), y, ks, vs, sems)

    state = (top.at[0], total.at[0], acc.at[0])
    state[0][...] = jnp.full((4 * QT, 128), NEG, jnp.float32)
    state[1][...] = jnp.zeros((4 * QT, 128), jnp.float32)
    state[2][...] = jnp.zeros((4 * QT, 128), jnp.float32)
    first = first_position(zh, y, tile)
    base = zh * (2048 // KT)

    @pl.loop(jnp.maximum(bounds[tile] // KT, base), (first + QT + KT - 1) // KT)
    def _(block):
        keys = pl.ds(aligned((block - base) * KT, KT), KT)
        edge = (block * KT + KT - 1 > first) | (block * KT < bounds[4 + tile])

        @pl.when(edge)
        def _():
            key_pos = block * KT + lax.broadcasted_iota(jnp.int32, (QT, KT), 1)
            query_pos = first + lax.broadcasted_iota(jnp.int32, (QT, KT), 0)
            mask = (key_pos <= query_pos) & (key_pos >= start_ref[:, :1])
            attend_step(stacked(q_ref), ks[keys, :], vs[keys, :], state, mask)

        @pl.when(jnp.logical_not(edge))
        def _():
            attend_step(stacked(q_ref), ks[keys, :], vs[keys, :], state, None)


def far_kernel(half, where, bounds, q_ref, start_ref, kv_z, kv_zy, *refs):
    top_in, total_in, acc_in, out_ref, ks, vs, top, total, acc, sems = refs
    zh, y = where[0], where[2]
    tile = 2 * half + pl.program_id(0)

    @pl.when((pl.program_id(0) == 0) & (zh == 1))
    def _():
        copy_keys((kv_z, kv_zy), y, ks, vs, sems)

    top[...] = top_in[0]
    total[...] = total_in[0]
    acc[...] = acc_in[0]

    @pl.loop(bounds[tile] // KT, zh * (2048 // KT))
    def _(block):
        keys = pl.ds(aligned(block * KT, KT), KT)
        edge = block * KT < bounds[4 + tile]

        @pl.when(edge)
        def _():
            key_pos = block * KT + lax.broadcasted_iota(jnp.int32, (QT, KT), 1)
            mask = key_pos >= start_ref[:, :1]
            attend_step(stacked(q_ref), ks[keys, :], vs[keys, :], (top, total, acc), mask)

        @pl.when(jnp.logical_not(edge))
        def _():
            attend_step(stacked(q_ref), ks[keys, :], vs[keys, :], (top, total, acc), None)

    result = acc[...] / jnp.sum(total[...], axis=1, keepdims=True)
    for h in range(4):
        out_ref[:, 128 * h : 128 * h + 128] = result[QT * h : QT * h + QT].astype(jnp.bfloat16)


def head_slot(where, dzl, dx, dc):
    return 4 * (where[1] ^ dzl) + 2 * (where[3] ^ dx) + (where[4] ^ dc)


def output_near_kernel(half, where, *refs):
    att_refs, wo_refs = refs[:6], refs[6:-4] if half == 0 else refs[6:7]
    zh, y = where[0], where[2]
    if half == 0:
        out_ref, wo, xs, sems = refs[-4:]
        copies = []
        for i, ref in enumerate(wo_refs):
            column = aligned((2 * (zh ^ (i // 2 % 2)) + (y ^ (i % 2))) * 128, 128)
            rows = slice(2048 * (i // 4), 2048 * (i // 4) + 2048)
            copies.append((ref, wo.at[rows, pl.ds(column, 128)]))
    else:
        out_ref, wo, xs, sems = refs[-4:]
        copies = [(wo_refs[0], wo)]
    slots = [head_slot(where, *at) for at in OFFSETS[:6]]
    for i, ref in enumerate(att_refs):
        copies.append((ref, xs.at[:, pl.ds(512 * i, 512)]))
    wait_all(start_copies(copies, sems))
    for n in range(2):
        columns = slice(256 * n, 256 * n + 256)
        acc = jnp.zeros((512, 256), jnp.float32)
        for i, slot in enumerate(slots):
            acc += jnp.dot(
                xs[:, 512 * i : 512 * i + 512],
                wo[pl.ds(aligned(slot * 512, 512), 512), columns],
                preferred_element_type=jnp.float32,
            )
        out_ref[:, columns] = acc


def output_far_kernel(where, *refs):
    far_refs, (wo_ref, part0, part1), (out_ref, xs, wo, sems) = refs[:4], refs[4:7], refs[7:]
    slots = [head_slot(where, *at) for at in OFFSETS[6:]]
    copies = []
    for half in range(2):
        for i in range(2):
            src = far_refs[2 * half + i]
            copies.append((src, xs.at[pl.ds(512 * half, 512), pl.ds(512 * i, 512)]))
    for i, slot in enumerate(slots):
        src = wo_ref.at[pl.ds(aligned(slot * 512, 512), 512), :]
        copies.append((src, wo.at[pl.ds(512 * i, 512), :]))
    wait_all(start_copies(copies, sems))
    for half, part in enumerate((part0, part1)):
        rows = slice(512 * half, 512 * half + 512)
        for n in range(2):
            columns = slice(256 * n, 256 * n + 256)
            acc = part[:, columns] + jnp.dot(
                xs[rows, :], wo[:, columns], preferred_element_type=jnp.float32
            )
            out_ref[rows, columns] = acc.astype(jnp.bfloat16)


def finish_kernel(tok_ref, sent_ref, out_ref):
    for block in range(32):
        zhp, zlp, yp, xp, cp = ((block >> s) & 1 for s in (4, 3, 2, 1, 0))
        source, part = 4 * zlp + 2 * xp + cp, 2 * zhp + yp
        columns = slice(128 * block, 128 * block + 128)
        sent = sent_ref[source, :, 128 * part : 128 * part + 128].astype(jnp.float32)
        out_ref[:, columns] = (tok_ref[:, columns].astype(jnp.float32) + sent).astype(jnp.bfloat16)


def call(kernel, out_shape, in_specs, scratch, cost, vmem=24, **more):
    flops, moved = cost
    more.setdefault("out_specs", jax.tree.map(lambda _: VMEM, out_shape))
    return pl.pallas_call(
        kernel,
        out_shape=out_shape,
        in_specs=in_specs,
        scratch_shapes=scratch,
        compiler_params=pltpu.CompilerParams(vmem_limit_bytes=vmem * 1024 * 1024),
        cost_estimate=pl.CostEstimate(flops=flops, bytes_accessed=moved, transcendentals=0),
        **more,
    )


def split_body(tokens, norm_gain, wq, wk, wv, wo, doc_ids):
    bf16, f32 = jnp.bfloat16, jnp.float32
    zh, zl, y, x, c = place = [lax.axis_index(axis) for axis in AXES]
    where = jnp.stack(place).astype(jnp.int32)

    weights = call(
        layout_kernel,
        jax.ShapeDtypeStruct((8, 128 + EXTRA, 768), bf16),
        [VMEM] * 4,
        [],
        (128 * EXTRA, 3 << 20),
    )(wq, wk, wv, doc_ids.reshape(1, 128))
    weights = lax.all_to_all(weights, QUAD, 0, 0, tiled=True)
    w_y = swap(weights, "y")
    wkv_z = swap(weights[:, :, 512:], "zh")
    wkv_zy = swap(wkv_z, "y")
    wq_z = [swap(weights[:, :128, 256 * n : 256 * n + 256], "zh") for n in range(2)]
    wq_zy = [swap(wq_z[n], "y") for n in range(2)]

    source = tokens.astype(f32)
    mean_sq = jnp.mean(source * source, axis=1, keepdims=True)
    normed = (source * lax.rsqrt(mean_sq + 1e-05) * norm_gain[None, :]).astype(bf16)
    tok_z = [swap(normed[64 * i : 64 * i + 64], "zl") for i in range(2)]
    tok_far = [swap(tok_z[i], "x") for i in range(2)]
    tok = []
    for piece in [normed, swap(normed, "x"), *tok_z, *tok_far]:
        tok += [piece, swap(piece, "c")]

    token = jnp.arange(1024, dtype=jnp.int32)
    positions = (2 * zh + token // 512) * 1024 + y * 512 + token % 512
    freqs = 500000.0 ** (-(jnp.arange(64, dtype=f32) * 2.0 / HEAD_WIDTH))
    angles = positions.astype(f32)[:, None] * freqs[None, :]
    cosine, sine = jnp.cos(angles), jnp.sin(angles)
    cosine = jnp.concatenate([cosine, cosine], axis=1)
    sine = jnp.concatenate([-sine, sine], axis=1)

    counts = jnp.concatenate(
        [piece[:, 128:, -128:] for piece in (weights, w_y, wkv_z, wkv_zy)], axis=0
    )

    keys_values, start_col, bounds = call(
        project_kv_kernel,
        (
            jax.ShapeDtypeStruct((1024, 256), bf16),
            jax.ShapeDtypeStruct((1024, 128), jnp.int32),
            jax.ShapeDtypeStruct((8,), jnp.int32),
        ),
        [SMEM, VMEM] + [ANY] * 16 + [VMEM, VMEM],
        [
            pltpu.VMEM((1024, 4096), bf16),
            pltpu.VMEM((32, 128, 256), bf16),
            pltpu.SemaphoreType.DMA((20,)),
        ],
        (2 * 1024 * 4096 * 256, 11 << 20),
        out_specs=(VMEM, VMEM, SMEM),
    )(where, counts, *tok, weights, w_y, wkv_z, wkv_zy, cosine, sine)
    queries = call(
        project_q_kernel,
        jax.ShapeDtypeStruct((1024, 512), bf16),
        [SMEM] + [ANY] * 18 + [VMEM, VMEM],
        [
            pltpu.VMEM((1024, 4096), bf16),
            pltpu.VMEM((32, 128, 512), bf16),
            pltpu.SemaphoreType.DMA((24,)),
        ],
        (2 * 1024 * 4096 * 512, 14 << 20),
    )(where, *tok, weights, w_y, *wq_z, *wq_zy, cosine, sine)

    kv_y = swap(keys_values, "y")
    kv_z = swap(keys_values, "zh")
    kv_zy = swap(kv_z, "y")

    def tile_spec(shape, first):
        return pl.BlockSpec(shape, lambda i: (i + first,) + (0,) * (len(shape) - 1))

    def state_specs():
        return [tile_spec((1, 4 * QT, 128), 0)] * 3

    def near_half(half):
        return call(
            functools.partial(near_kernel, half),
            [jax.ShapeDtypeStruct((2, 4 * QT, 128), f32)] * 3,
            [SMEM] * 2
            + [tile_spec((QT, 512), 2 * half), tile_spec((QT, 128), 2 * half), ANY, ANY],
            [
                pltpu.VMEM((2048, 128), bf16),
                pltpu.VMEM((2048, 128), bf16),
                pltpu.SemaphoreType.DMA((8,)),
            ],
            (4 * 512 * 2048 * 512, 4 << 20),
            grid=(2,),
            out_specs=state_specs(),
        )(where, bounds, queries, start_col, keys_values, kv_y)

    state = [near_half(0), near_half(1)]

    def far_call(half):
        return call(
            functools.partial(far_kernel, half),
            jax.ShapeDtypeStruct((512, 512), bf16),
            [SMEM, SMEM, tile_spec((QT, 512), 2 * half), tile_spec((QT, 128), 2 * half)]
            + [ANY, ANY] + state_specs(),
            [
                pltpu.VMEM((2048, 128), bf16),
                pltpu.VMEM((2048, 128), bf16),
                pltpu.VMEM((4 * QT, 128), f32),
                pltpu.VMEM((4 * QT, 128), f32),
                pltpu.VMEM((4 * QT, 128), f32),
                pltpu.SemaphoreType.DMA((8,)),
            ],
            (4 * 512 * 2048 * 512, 8 << 20),
            grid=(2,),
            out_specs=pl.BlockSpec((QT, 512), lambda i: (i, 0)),
        )(where, bounds, queries, start_col, kv_z, kv_zy, *state[half])

    attended = [far_call(0), far_call(1)]

    wos = []
    for part in range(2):
        piece = wo[2048 * part : 2048 * part + 2048]
        by_z = swap(piece, "zh")
        wos += [piece, swap(piece, "y"), by_z, swap(by_z, "y")]

    att = [quad_gather(attended[half], half == 1) for half in range(2)]

    def output_near(half, weights):
        rows = jax.ShapeDtypeStruct((512, 512), f32)
        laid = jax.ShapeDtypeStruct((4096, 512), bf16)
        return call(
            functools.partial(output_near_kernel, half),
            [rows, laid] if half == 0 else [rows],
            [SMEM] + [ANY] * (6 + len(weights)),
            ([] if half == 0 else [pltpu.VMEM((4096, 512), bf16)])
            + [pltpu.VMEM((512, 3072), bf16), pltpu.SemaphoreType.DMA((14,))],
            (2 * 512 * 3072 * 512, 9 << 20),
        )(where, *[att[half][at] for at in OFFSETS[:6]], *weights)

    part0, laid = output_near(0, wos)
    (part1,) = output_near(1, [laid])
    sent = call(
        output_far_kernel,
        jax.ShapeDtypeStruct((1024, 512), bf16),
        [SMEM] + [ANY] * 5 + [VMEM] * 2,
        [
            pltpu.VMEM((1024, 1024), bf16),
            pltpu.VMEM((1024, 512), bf16),
            pltpu.SemaphoreType.DMA((6,)),
        ],
        (2 * 1024 * 1024 * 512, 5 << 20),
    )(where, *[att[half][at] for half in range(2) for at in OFFSETS[6:]], laid, part0, part1)
    home = lax.all_to_all(sent.reshape(8, 128, 512), QUAD, 0, 0, tiled=True)
    return call(
        finish_kernel,
        jax.ShapeDtypeStruct((128, 4096), bf16),
        [VMEM, VMEM],
        [],
        (128 * 4096, 3 << 20),
    )(tokens, home)


def rope(field, positions):
    half = field.shape[-1] // 2
    freqs = 500000.0 ** (-(jnp.arange(half, dtype=jnp.float32) * 2.0 / field.shape[-1]))
    angles = positions.astype(jnp.float32)[:, None] * freqs[None, :]
    cosine = jnp.cos(angles)[:, None, :]
    sine = jnp.sin(angles)[:, None, :]
    first = field[..., :half]
    second = field[..., half:]
    return jnp.concatenate(
        [first * cosine - second * sine, second * cosine + first * sine], axis=-1
    )


def local(tokens, norm_gain, wq, wk, wv, wo, doc_ids):
    tok_rows = tokens.shape[0]
    head_size = HEAD_WIDTH
    kv_local = wk.shape[1] // head_size
    query_group = QUERY_HEADS // KV_HEAD_COUNT
    source = tokens.astype(jnp.float32)
    whole = lax.all_gather(tokens, "head", axis=1, tiled=True).astype(jnp.float32)
    mean_sq = jnp.mean(whole * whole, axis=1, keepdims=True)
    normed_input = (whole * lax.rsqrt(mean_sq + 1e-05) * norm_gain[None, :]).astype(jnp.bfloat16)
    query_acc = jnp.dot(
        normed_input,
        lax.all_gather(wq, ("seq", "srv"), axis=0, tiled=True),
        preferred_element_type=jnp.float32,
    )
    key_acc = jnp.dot(
        normed_input,
        lax.all_gather(wk, ("seq", "srv"), axis=0, tiled=True),
        preferred_element_type=jnp.float32,
    )
    value_acc = jnp.dot(
        normed_input,
        lax.all_gather(wv, ("seq", "srv"), axis=0, tiled=True),
        preferred_element_type=jnp.float32,
    )
    first_pos = lax.axis_index(("seq", "srv")) * tok_rows
    positions = first_pos + jnp.arange(tok_rows, dtype=jnp.int32)
    query_matrix = rope(query_acc.reshape(tok_rows, kv_local * query_group, head_size), positions)
    query_matrix = query_matrix.astype(jnp.bfloat16).reshape(
        tok_rows, kv_local, query_group, head_size
    )
    key_matrix = rope(key_acc.reshape(tok_rows, kv_local, head_size), positions).astype(
        jnp.bfloat16
    )
    key_matrix = key_matrix.reshape(tok_rows, kv_local * head_size)
    value_matrix = value_acc.astype(jnp.bfloat16)
    scale = 1.0 / head_size**0.5

    def attend_block(carry, key_rows, value_rows, doc_rows, key_pos):
        run_top, run_total, run_acc = carry
        key_heads = key_rows.reshape(key_rows.shape[0], kv_local, head_size)
        value_heads = value_rows.reshape(value_rows.shape[0], kv_local, head_size)
        scores = (
            jnp.einsum(
                "qcgd,kcd->qcgk", query_matrix, key_heads, preferred_element_type=jnp.float32
            )
            * scale
        )
        allowed = (
            (key_pos[None, :] <= positions[:, None])
            & (key_pos[None, :] >= 0)
            & (doc_rows[None, :] == doc_ids[:, None])
        )
        allowed = allowed[:, None, None, :]
        masked = jnp.where(allowed, scores, -1e30)
        new_top = jnp.maximum(run_top, jnp.max(masked, axis=3))
        expd = jnp.where(allowed, jnp.exp(masked - new_top[..., None]), 0.0)
        factor = jnp.exp(run_top - new_top)
        new_total = run_total * factor + jnp.sum(expd, axis=3)
        weights = expd.astype(jnp.bfloat16)
        update = jnp.einsum(
            "qcgk,kcd->qcgd", weights, value_heads, preferred_element_type=jnp.float32
        )
        return (new_top, new_total, run_acc * factor[..., None] + update)

    start_state = (
        jnp.full((tok_rows, kv_local, query_group), -1e30, jnp.float32),
        jnp.zeros((tok_rows, kv_local, query_group), jnp.float32),
        jnp.zeros((tok_rows, kv_local, query_group, head_size), jnp.float32),
    )
    key_piece = lax.all_gather(key_matrix, ("seq", "srv"), axis=0, tiled=True)
    value_piece = lax.all_gather(value_matrix, ("seq", "srv"), axis=0, tiled=True)
    doc_piece = lax.all_gather(doc_ids, ("seq", "srv"), axis=0, tiled=True)
    count = key_piece.shape[0]
    width = math.gcd(count, 512)

    def step(inner, index):
        offset = index * width
        key_rows = lax.dynamic_slice_in_dim(key_piece, offset, width, 0)
        value_rows = lax.dynamic_slice_in_dim(value_piece, offset, width, 0)
        doc_rows = lax.dynamic_slice_in_dim(doc_piece, offset, width, 0)
        key_pos = offset + jnp.arange(width, dtype=jnp.int32)
        return (attend_block(inner, key_rows, value_rows, doc_rows, key_pos), None)

    def run_all(inner):
        result, _ = lax.scan(step, inner, jnp.arange(count // width, dtype=jnp.int32))
        return result

    beyond = jnp.int32(0) > first_pos + tok_rows - 1
    before = doc_piece[count - 1] < doc_ids[0]
    _, final_total, final_acc = lax.cond(beyond | before, lambda inner: inner, run_all, start_state)
    attended = (final_acc / final_total[..., None]).astype(jnp.bfloat16)
    attended = attended.reshape(tok_rows, kv_local * query_group * head_size)
    terms = jnp.dot(
        attended,
        lax.all_gather(wo, ("seq", "srv"), axis=1, tiled=True),
        preferred_element_type=jnp.float32,
    )
    summed = lax.psum_scatter(
        terms.astype(jnp.bfloat16), "head", scatter_dimension=1, tiled=True
    ).astype(jnp.float32)
    return (source + summed).astype(jnp.bfloat16)


def solution(mesh):
    sizes = dict(mesh.shape)
    if sizes["grp"] == 1 and sizes["head"] == 1 and sizes["seq"] == 16 and sizes["srv"] == 2:
        fine = Mesh(np.asarray(mesh.devices).reshape(2, 2, 2, 2, 2), AXES)
        in_specs = (P(AXES), P(), P(AXES), P(AXES), P(AXES), P(None, AXES), P(AXES))
        return jax.shard_map(
            split_body, mesh=fine, in_specs=in_specs, out_specs=P(AXES), check_vma=False
        )
    in_specs = (
        P(("grp", "seq", "srv"), "head"),
        P(),
        P(("seq", "srv"), "head"),
        P(("seq", "srv"), "head"),
        P(("seq", "srv"), "head"),
        P("head", ("seq", "srv")),
        P(("grp", "seq", "srv")),
    )
    out_specs = P(("grp", "seq", "srv"), "head")
    return jax.shard_map(local, mesh=mesh, in_specs=in_specs, out_specs=out_specs, check_vma=False)
```

```python
import functools
import math

import jax
import jax.numpy as jnp
import numpy as np
from jax import lax
from jax.experimental import pallas as pl
from jax.experimental.pallas import tpu as pltpu
from jax.sharding import Mesh
from jax.sharding import PartitionSpec as P

QUERY_HEADS = 32
KV_HEAD_COUNT = 8
HEAD_WIDTH = 128
DOCS = 8


AXES = ("zh", "zl", "y", "x", "c")
QUAD = ("zl", "x", "c")
SWAP = [(0, 1), (1, 0)]
EXTRA = 8
QT = 256
KT = 512
NEG = -1e30

ANY = pl.BlockSpec(memory_space=pl.ANY)
VMEM = pl.BlockSpec(memory_space=pltpu.VMEM)
SMEM = pl.BlockSpec(memory_space=pltpu.SMEM)
HBM = pl.BlockSpec(memory_space=pltpu.HBM)


def swap(value, axis):
    return lax.ppermute(value, axis, SWAP)


def quad_gather(block, by_z_first):
    by_x = swap(block, "x")
    by_z = swap(block, "zl")
    far = swap(by_z, "x") if by_z_first else swap(by_x, "zl")
    got = {(0, 0): block, (0, 1): by_x, (1, 0): by_z, (1, 1): far}
    out = {}
    for (dzl, dx), piece in got.items():
        out[dzl, dx, 0] = piece
        out[dzl, dx, 1] = swap(piece, "c")
    return out


OFFSETS = [(dzl, dx, dc) for dzl in range(2) for dx in range(2) for dc in range(2)]


def start_copies(copies, sems, first=0):
    started = []
    for i, (src, dst) in enumerate(copies):
        copy = pltpu.make_async_copy(src, dst, sems.at[first + i])
        copy.start()
        started.append(copy)
    return started


def wait_all(copies):
    for copy in copies:
        copy.wait()


def aligned(value, step):
    return pl.multiple_of(value, step)


def layout_kernel(wq_ref, wk_ref, wv_ref, doc_ref, out_ref, sems):
    copies = []
    for j in range(8):
        for ref, first, size in ((wq_ref, 0, 512), (wk_ref, 512, 128), (wv_ref, 640, 128)):
            target = out_ref.at[j, pl.ds(0, 128), pl.ds(first, size)]
            copies.append((ref.at[:, pl.ds(size * j, size)], target))
    started = start_copies(copies, sems)
    below = doc_ref[...] < lax.broadcasted_iota(jnp.int32, (EXTRA, 128), 0)
    count = jnp.sum(jnp.where(below, 1.0, 0.0), axis=1, keepdims=True)
    rows = jnp.broadcast_to(count, (EXTRA, 768)).astype(jnp.bfloat16)
    for j in range(8):
        out_ref[j, 128:, :] = rows
    wait_all(started)


TOKEN_PIECES = [
    (dzl, dx, dc, first, rows)
    for dzl, dx, first, rows in (
        (0, 0, 0, 128),
        (0, 1, 0, 128),
        (1, 0, 0, 64),
        (1, 0, 64, 64),
        (1, 1, 0, 64),
        (1, 1, 64, 64),
    )
    for dc in range(2)
]


def token_copies(dzl, where, tok_refs, xs):
    zl, x, c = where[1], where[3], where[4]
    copies = []
    for (piece_dzl, dx, dc, first, rows), ref in zip(TOKEN_PIECES, tok_refs):
        if piece_dzl == dzl:
            slot = 4 * (zl ^ dzl) + 2 * (x ^ dx) + (c ^ dc)
            copies.append((ref, xs.at[pl.ds(aligned(slot * 128 + first, 64), rows), :]))
    return copies


def weight_copies(where, pieces, dst):
    copies = []
    for dzh, dy, ref, source, target in pieces:
        for zlp in range(2):
            block = 4 * (where[0] ^ dzh) + 2 * zlp + (where[2] ^ dy)
            src = ref.at[pl.ds(4 * zlp, 4), pl.ds(0, 128), source]
            copies.append((src, dst.at[pl.ds(4 * block, 4), :, target]))
    return copies


def turn(part, cos_ref, sin_ref, rows):
    return part * cos_ref[rows, :] + pltpu.roll(part, 64, axis=1) * sin_ref[rows, :]


def project_kv_kernel(where, count_ref, *refs):
    tok_refs, (w_own, w_y, w_z, w_zy, cos_ref, sin_ref) = refs[:12], refs[12:18]
    kv_out, start_out, bounds_out, xs, wkv, sems = refs[18:]
    zh, zl, y = where[0], where[1], where[2]
    columns, whole = pl.ds(512, 256), pl.ds(0, 256)
    near = start_copies(token_copies(0, where, tok_refs, xs), sems)
    pieces = (
        (0, 0, w_own, columns, whole),
        (0, 1, w_y, columns, whole),
        (1, 0, w_z, whole, whole),
        (1, 1, w_zy, whole, whole),
    )
    near += start_copies(weight_copies(where, pieces, wkv), sems, 4)
    far = start_copies(token_copies(1, where, tok_refs, xs), sems, 12)

    counts = jnp.sum(count_ref[...].astype(jnp.float32), axis=0).astype(jnp.int32)
    for half in range(2):
        base = (2 * zh + half) * 1024 + y * 512
        position = base + lax.broadcasted_iota(jnp.int32, (512, 128), 0)
        start = jnp.zeros((512, 128), jnp.int32)
        for d in range(DOCS):
            row = counts[d : d + 1, :]
            start = jnp.maximum(start, jnp.where(position >= row, row, 0))
        start_out[512 * half : 512 * half + 512, :] = start
    document = [jnp.max(counts[d : d + 1, :]) for d in range(DOCS)]
    for tile in range(1024 // QT):
        first = first_position(zh, y, tile)
        for k, position in enumerate((first, first + QT - 1)):
            bound = jnp.int32(0)
            for d in range(DOCS):
                bound = jnp.maximum(bound, jnp.where(position >= document[d], document[d], 0))
            bounds_out[4 * k + tile] = bound

    for dzl, waits in enumerate((near, far)):
        wait_all(waits)
        rows = pl.ds(aligned((zl ^ dzl) * 512, 512), 512)
        weights = wkv[...].reshape(4096, 256)
        acc = jnp.dot(xs[rows, :], weights, preferred_element_type=jnp.float32)
        kv_out[rows, :128] = turn(acc[:, :128], cos_ref, sin_ref, rows).astype(jnp.bfloat16)
        kv_out[rows, 128:] = acc[:, 128:].astype(jnp.bfloat16)


def project_q_kernel(where, *refs):
    tok_refs = refs[:12]
    w_own, w_y, w_z0, w_z1, w_z2, w_zy0, cos_ref, sin_ref = refs[12:20]
    q_out, part_out, xs, wq, sems = refs[20:]
    whole, left = pl.ds(0, 512), pl.ds(0, 256)
    slim = pl.ds(0, 128)
    near = start_copies(token_copies(0, where, tok_refs, xs), sems)
    pieces = (
        (0, 0, w_own, whole, whole),
        (0, 1, w_y, whole, whole),
        (1, 0, w_z0, left, left),
        (1, 0, w_z1, slim, pl.ds(256, 128)),
        (1, 0, w_z2, slim, pl.ds(384, 128)),
        (1, 1, w_zy0, left, left),
    )
    near += start_copies(weight_copies(where, pieces, wq), sems, 4)
    far = start_copies(token_copies(1, where, tok_refs, xs), sems, 16)
    for zlp in range(2):
        block = 4 * (where[0] ^ 1) + 2 * zlp + (where[2] ^ 1)
        wq[pl.ds(4 * block, 4), :, 256:] = jnp.zeros((4, 128, 256), jnp.bfloat16)
    for dzl, waits in enumerate((near, far)):
        wait_all(waits)
        rows = pl.ds(aligned((where[1] ^ dzl) * 512, 512), 512)
        weights = wq[:, :, :256].reshape(4096, 256)
        acc = jnp.dot(xs[rows, :], weights, preferred_element_type=jnp.float32)
        for k in range(2):
            columns = slice(128 * k, 128 * k + 128)
            part = turn(acc[:, columns], cos_ref, sin_ref, rows)
            q_out[rows, columns] = part.astype(jnp.bfloat16)
        weights = wq[:, :, 256:].reshape(4096, 256)
        part_out[rows, :] = jnp.dot(xs[rows, :], weights, preferred_element_type=jnp.float32)


def project_rest_kernel(where, *refs):
    tok_refs, (w_zy1, w_zy2, part_ref, cos_ref, sin_ref) = refs[:12], refs[12:17]
    q_out, xs, wq, sems = refs[17:]
    copies = [(w_zy1, wq.at[:, :, pl.ds(0, 128)]), (w_zy2, wq.at[:, :, pl.ds(128, 128)])]
    for dzl in range(2):
        for ref, target in token_copies(dzl, where, tok_refs, xs):
            copies.append((ref, target))
    split = copies[:2]
    for ref, target in copies[2:]:
        for zlp in range(2):
            block = 4 * (where[0] ^ 1) + 2 * zlp + (where[2] ^ 1)
            source = ref.at[:, pl.ds(aligned(block * 512, 512), 512)]
            split.append((source, target.at[:, pl.ds(512 * zlp, 512)]))
    wait_all(start_copies(split, sems))
    acc = part_ref[...] + jnp.dot(
        xs[...], wq[...].reshape(1024, 256), preferred_element_type=jnp.float32
    )
    for k in range(2):
        columns = slice(128 * k, 128 * k + 128)
        part = turn(acc[:, columns], cos_ref, sin_ref, slice(None))
        q_out[:, columns] = part.astype(jnp.bfloat16)


FACTOR = math.log2(math.e) / math.sqrt(HEAD_WIDTH)


def first_position(zh, y, tile):
    return (2 * zh + tile // 2) * 1024 + y * 512 + (tile % 2) * QT


def copy_keys(kv_refs, y, ks, vs, sems):
    copies = []
    for dy, ref in enumerate(kv_refs):
        for zlp in range(2):
            row = aligned((2 * zlp + (y ^ dy)) * 512, 512)
            for half, dst in ((0, ks), (1, vs)):
                src = ref.at[pl.ds(zlp * 512, 512), pl.ds(half * 128, 128)]
                copies.append((src, dst.at[pl.ds(row, 512), :]))
    wait_all(start_copies(copies, sems))


def attend_step(queries, keys, values, state, mask):
    top, total, acc = state
    scores = lax.dot_general(
        queries, keys, (((1,), (1,)), ((), ())), preferred_element_type=jnp.float32
    )
    if mask is not None:
        scores = jnp.where(mask[None], scores.reshape(4, QT, KT), NEG).reshape(4 * QT, KT)
    cuts = [slice(128 * i, 128 * i + 128) for i in range(KT // 128)]
    best = functools.reduce(jnp.maximum, [scores[:, cut] for cut in cuts])
    old = top[...]
    new = jnp.maximum(old, jnp.max(best, axis=1, keepdims=True))
    top[...] = new
    shrink = jnp.exp2((old - new) * FACTOR)
    parts = [jnp.exp2((scores[:, cut] - new) * FACTOR) for cut in cuts]
    total[...] = total[...] * shrink + functools.reduce(jnp.add, parts)
    weights = jnp.concatenate([part.astype(jnp.bfloat16) for part in parts], axis=1)
    acc[...] = acc[...] * shrink + jnp.dot(weights, values, preferred_element_type=jnp.float32)


def stacked(*q_refs):
    return jnp.concatenate([ref[:, 128 * h : 128 * h + 128] for ref in q_refs for h in range(2)])


def near_kernel(half, where, bounds, q_ref, q2_ref, start_ref, kv_own, kv_y, *refs):
    top, total, acc, ks, vs, sems = refs
    zh, y = where[0], where[2]
    tile = 2 * half + pl.program_id(0)

    @pl.when(pl.program_id(0) == 0)
    def _():
        copy_keys((kv_own, kv_y), y, ks, vs, sems)

    state = (top.at[0], total.at[0], acc.at[0])
    state[0][...] = jnp.full((4 * QT, 128), NEG, jnp.float32)
    state[1][...] = jnp.zeros((4 * QT, 128), jnp.float32)
    state[2][...] = jnp.zeros((4 * QT, 128), jnp.float32)
    first = first_position(zh, y, tile)
    base = zh * (2048 // KT)

    @pl.loop(jnp.maximum(bounds[tile] // KT, base), (first + QT + KT - 1) // KT)
    def _(block):
        keys = pl.ds(aligned((block - base) * KT, KT), KT)
        edge = (block * KT + KT - 1 > first) | (block * KT < bounds[4 + tile])

        @pl.when(edge)
        def _():
            key_pos = block * KT + lax.broadcasted_iota(jnp.int32, (QT, KT), 1)
            query_pos = first + lax.broadcasted_iota(jnp.int32, (QT, KT), 0)
            mask = (key_pos <= query_pos) & (key_pos >= start_ref[:, :1])
            attend_step(stacked(q_ref, q2_ref), ks[keys, :], vs[keys, :], state, mask)

        @pl.when(jnp.logical_not(edge))
        def _():
            attend_step(stacked(q_ref, q2_ref), ks[keys, :], vs[keys, :], state, None)


def far_kernel(half, where, bounds, q_ref, q2_ref, start_ref, kv_z, kv_zy, *refs):
    top_in, total_in, acc_in, out_ref, ks, vs, top, total, acc, sems = refs
    zh, y = where[0], where[2]
    tile = 2 * half + pl.program_id(0)

    @pl.when((pl.program_id(0) == 0) & (zh == 1))
    def _():
        copy_keys((kv_z, kv_zy), y, ks, vs, sems)

    top[...] = top_in[0]
    total[...] = total_in[0]
    acc[...] = acc_in[0]

    @pl.loop(bounds[tile] // KT, zh * (2048 // KT))
    def _(block):
        keys = pl.ds(aligned(block * KT, KT), KT)
        edge = block * KT < bounds[4 + tile]

        @pl.when(edge)
        def _():
            key_pos = block * KT + lax.broadcasted_iota(jnp.int32, (QT, KT), 1)
            mask = key_pos >= start_ref[:, :1]
            attend_step(stacked(q_ref, q2_ref), ks[keys, :], vs[keys, :], (top, total, acc), mask)

        @pl.when(jnp.logical_not(edge))
        def _():
            attend_step(stacked(q_ref, q2_ref), ks[keys, :], vs[keys, :], (top, total, acc), None)

    result = acc[...] / jnp.sum(total[...], axis=1, keepdims=True)
    for h in range(4):
        out_ref[:, 128 * h : 128 * h + 128] = result[QT * h : QT * h + QT].astype(jnp.bfloat16)


def head_slot(where, dzl, dx, dc):
    return 4 * (where[1] ^ dzl) + 2 * (where[3] ^ dx) + (where[4] ^ dc)


def output_near_kernel(half, where, *refs):
    att_refs, wo_refs = refs[:6], refs[6:-4] if half == 0 else refs[6:7]
    zh, y = where[0], where[2]
    if half == 0:
        out_ref, wo, xs, sems = refs[-4:]
        copies = []
        for i, ref in enumerate(wo_refs):
            column = aligned((2 * (zh ^ (i // 2 % 2)) + (y ^ (i % 2))) * 128, 128)
            rows = slice(2048 * (i // 4), 2048 * (i // 4) + 2048)
            copies.append((ref, wo.at[rows, pl.ds(column, 128)]))
    else:
        out_ref, wo, xs, sems = refs[-4:]
        copies = [(wo_refs[0], wo)]
    slots = [head_slot(where, *at) for at in OFFSETS[:6]]
    for i, ref in enumerate(att_refs):
        copies.append((ref, xs.at[:, pl.ds(512 * i, 512)]))
    wait_all(start_copies(copies, sems))
    for n in range(2):
        columns = slice(256 * n, 256 * n + 256)
        acc = jnp.zeros((512, 256), jnp.float32)
        for i, slot in enumerate(slots):
            acc += jnp.dot(
                xs[:, 512 * i : 512 * i + 512],
                wo[pl.ds(aligned(slot * 512, 512), 512), columns],
                preferred_element_type=jnp.float32,
            )
        out_ref[:, columns] = acc


def output_far_kernel(where, *refs):
    far_refs, (wo_ref, part0, part1), (out_ref, xs, wo, sems) = refs[:4], refs[4:7], refs[7:]
    slots = [head_slot(where, *at) for at in OFFSETS[6:]]
    copies = []
    for half in range(2):
        for i in range(2):
            src = far_refs[2 * half + i]
            copies.append((src, xs.at[pl.ds(512 * half, 512), pl.ds(512 * i, 512)]))
    for i, slot in enumerate(slots):
        src = wo_ref.at[pl.ds(aligned(slot * 512, 512), 512), :]
        copies.append((src, wo.at[pl.ds(512 * i, 512), :]))
    wait_all(start_copies(copies, sems))
    for half, part in enumerate((part0, part1)):
        rows = slice(512 * half, 512 * half + 512)
        for n in range(2):
            columns = slice(256 * n, 256 * n + 256)
            acc = part[:, columns] + jnp.dot(
                xs[rows, :], wo[:, columns], preferred_element_type=jnp.float32
            )
            out_ref[rows, columns] = acc.astype(jnp.bfloat16)


def finish_kernel(tok_ref, sent_ref, out_ref):
    for block in range(32):
        zhp, zlp, yp, xp, cp = ((block >> s) & 1 for s in (4, 3, 2, 1, 0))
        source, part = 4 * zlp + 2 * xp + cp, 2 * zhp + yp
        columns = slice(128 * block, 128 * block + 128)
        sent = sent_ref[source, :, 128 * part : 128 * part + 128].astype(jnp.float32)
        out_ref[:, columns] = (tok_ref[:, columns].astype(jnp.float32) + sent).astype(jnp.bfloat16)


def call(kernel, out_shape, in_specs, scratch, cost, vmem=24, **more):
    flops, moved = cost
    more.setdefault("out_specs", jax.tree.map(lambda _: VMEM, out_shape))
    return pl.pallas_call(
        kernel,
        out_shape=out_shape,
        in_specs=in_specs,
        scratch_shapes=scratch,
        compiler_params=pltpu.CompilerParams(vmem_limit_bytes=vmem * 1024 * 1024),
        cost_estimate=pl.CostEstimate(flops=flops, bytes_accessed=moved, transcendentals=0),
        **more,
    )


def split_body(tokens, norm_gain, wq, wk, wv, wo, doc_ids):
    bf16, f32 = jnp.bfloat16, jnp.float32
    zh, zl, y, x, c = place = [lax.axis_index(axis) for axis in AXES]
    where = jnp.stack(place).astype(jnp.int32)

    weights = call(
        layout_kernel,
        jax.ShapeDtypeStruct((8, 128 + EXTRA, 768), bf16),
        [HBM] * 3 + [VMEM],
        [pltpu.SemaphoreType.DMA((24,))],
        (128 * EXTRA, 3 << 20),
    )(wq, wk, wv, doc_ids.reshape(1, 128))
    weights = lax.all_to_all(weights, QUAD, 0, 0, tiled=True)
    w_y = swap(weights, "y")
    wkv_z = swap(weights[:, :, 512:], "zh")
    wkv_zy = swap(wkv_z, "y")
    cuts = [slice(0, 256), slice(256, 384), slice(384, 512)]
    wq_z = [swap(weights[:, :128, cut], "zh") for cut in cuts]
    wq_zy = [swap(piece, "y") for piece in wq_z]

    source = tokens.astype(f32)
    mean_sq = jnp.mean(source * source, axis=1, keepdims=True)
    normed = (source * lax.rsqrt(mean_sq + 1e-05) * norm_gain[None, :]).astype(bf16)
    tok_z = [swap(normed[64 * i : 64 * i + 64], "zl") for i in range(2)]
    tok_far = [swap(tok_z[i], "x") for i in range(2)]
    tok = []
    for piece in [normed, swap(normed, "x"), *tok_z, *tok_far]:
        tok += [piece, swap(piece, "c")]

    token = jnp.arange(1024, dtype=jnp.int32)
    positions = (2 * zh + token // 512) * 1024 + y * 512 + token % 512
    freqs = 500000.0 ** (-(jnp.arange(64, dtype=f32) * 2.0 / HEAD_WIDTH))
    angles = positions.astype(f32)[:, None] * freqs[None, :]
    cosine, sine = jnp.cos(angles), jnp.sin(angles)
    cosine = jnp.concatenate([cosine, cosine], axis=1)
    sine = jnp.concatenate([-sine, sine], axis=1)

    counts = jnp.concatenate(
        [piece[:, 128:, -128:] for piece in (weights, w_y, wkv_z, wkv_zy)], axis=0
    )

    keys_values, start_col, bounds = call(
        project_kv_kernel,
        (
            jax.ShapeDtypeStruct((1024, 256), bf16),
            jax.ShapeDtypeStruct((1024, 128), jnp.int32),
            jax.ShapeDtypeStruct((8,), jnp.int32),
        ),
        [SMEM, VMEM] + [ANY] * 16 + [VMEM, VMEM],
        [
            pltpu.VMEM((1024, 4096), bf16),
            pltpu.VMEM((32, 128, 256), bf16),
            pltpu.SemaphoreType.DMA((20,)),
        ],
        (2 * 1024 * 4096 * 256, 11 << 20),
        out_specs=(VMEM, VMEM, SMEM),
    )(where, counts, *tok, weights, w_y, wkv_z, wkv_zy, cosine, sine)
    first_queries, part = call(
        project_q_kernel,
        (jax.ShapeDtypeStruct((1024, 256), bf16), jax.ShapeDtypeStruct((1024, 256), f32)),
        [SMEM] + [ANY] * 18 + [VMEM, VMEM],
        [
            pltpu.VMEM((1024, 4096), bf16),
            pltpu.VMEM((32, 128, 512), bf16),
            pltpu.SemaphoreType.DMA((24,)),
        ],
        (2 * 1024 * 4096 * 512, 14 << 20),
    )(where, *tok, weights, w_y, *wq_z, wq_zy[0], cosine, sine)
    rest_queries = call(
        project_rest_kernel,
        jax.ShapeDtypeStruct((1024, 256), bf16),
        [SMEM] + [ANY] * 14 + [VMEM] * 3,
        [
            pltpu.VMEM((1024, 1024), bf16),
            pltpu.VMEM((8, 128, 256), bf16),
            pltpu.SemaphoreType.DMA((26,)),
        ],
        (2 * 1024 * 1024 * 256, 5 << 20),
    )(where, *tok, *wq_zy[1:], part, cosine, sine)
    queries = (first_queries, rest_queries)

    kv_y = swap(keys_values, "y")
    kv_z = swap(keys_values, "zh")
    kv_zy = swap(kv_z, "y")

    def tile_spec(shape, first):
        return pl.BlockSpec(shape, lambda i: (i + first,) + (0,) * (len(shape) - 1))

    def state_specs():
        return [tile_spec((1, 4 * QT, 128), 0)] * 3

    def near_half(half):
        return call(
            functools.partial(near_kernel, half),
            [jax.ShapeDtypeStruct((2, 4 * QT, 128), f32)] * 3,
            [SMEM] * 2
            + [tile_spec((QT, 256), 2 * half), tile_spec((QT, 256), 2 * half),
            tile_spec((QT, 128), 2 * half), ANY, ANY],
            [
                pltpu.VMEM((2048, 128), bf16),
                pltpu.VMEM((2048, 128), bf16),
                pltpu.SemaphoreType.DMA((8,)),
            ],
            (4 * 512 * 2048 * 512, 4 << 20),
            grid=(2,),
            out_specs=state_specs(),
        )(where, bounds, *queries, start_col, keys_values, kv_y)

    state = [near_half(0), near_half(1)]

    def far_call(half):
        return call(
            functools.partial(far_kernel, half),
            jax.ShapeDtypeStruct((512, 512), bf16),
            [SMEM, SMEM, tile_spec((QT, 256), 2 * half), tile_spec((QT, 256), 2 * half),
                tile_spec((QT, 128), 2 * half)]
            + [ANY, ANY] + state_specs(),
            [
                pltpu.VMEM((2048, 128), bf16),
                pltpu.VMEM((2048, 128), bf16),
                pltpu.VMEM((4 * QT, 128), f32),
                pltpu.VMEM((4 * QT, 128), f32),
                pltpu.VMEM((4 * QT, 128), f32),
                pltpu.SemaphoreType.DMA((8,)),
            ],
            (4 * 512 * 2048 * 512, 8 << 20),
            grid=(2,),
            out_specs=pl.BlockSpec((QT, 512), lambda i: (i, 0)),
        )(where, bounds, *queries, start_col, kv_z, kv_zy, *state[half])

    attended = [far_call(0), far_call(1)]

    wos = []
    for part in range(2):
        piece = wo[2048 * part : 2048 * part + 2048]
        by_z = swap(piece, "zh")
        wos += [piece, swap(piece, "y"), by_z, swap(by_z, "y")]

    att = [quad_gather(attended[half], half == 1) for half in range(2)]

    def output_near(half, weights):
        rows = jax.ShapeDtypeStruct((512, 512), f32)
        laid = jax.ShapeDtypeStruct((4096, 512), bf16)
        return call(
            functools.partial(output_near_kernel, half),
            [rows, laid] if half == 0 else [rows],
            [SMEM] + [ANY] * (6 + len(weights)),
            ([] if half == 0 else [pltpu.VMEM((4096, 512), bf16)])
            + [pltpu.VMEM((512, 3072), bf16), pltpu.SemaphoreType.DMA((14,))],
            (2 * 512 * 3072 * 512, 9 << 20),
        )(where, *[att[half][at] for at in OFFSETS[:6]], *weights)

    part0, laid = output_near(0, wos)
    (part1,) = output_near(1, [laid])
    sent = call(
        output_far_kernel,
        jax.ShapeDtypeStruct((1024, 512), bf16),
        [SMEM] + [ANY] * 5 + [VMEM] * 2,
        [
            pltpu.VMEM((1024, 1024), bf16),
            pltpu.VMEM((1024, 512), bf16),
            pltpu.SemaphoreType.DMA((6,)),
        ],
        (2 * 1024 * 1024 * 512, 5 << 20),
    )(where, *[att[half][at] for half in range(2) for at in OFFSETS[6:]], laid, part0, part1)
    home = lax.all_to_all(sent.reshape(8, 128, 512), QUAD, 0, 0, tiled=True)
    return call(
        finish_kernel,
        jax.ShapeDtypeStruct((128, 4096), bf16),
        [VMEM, VMEM],
        [],
        (128 * 4096, 3 << 20),
    )(tokens, home)


def rope(field, positions):
    half = field.shape[-1] // 2
    freqs = 500000.0 ** (-(jnp.arange(half, dtype=jnp.float32) * 2.0 / field.shape[-1]))
    angles = positions.astype(jnp.float32)[:, None] * freqs[None, :]
    cosine = jnp.cos(angles)[:, None, :]
    sine = jnp.sin(angles)[:, None, :]
    first = field[..., :half]
    second = field[..., half:]
    return jnp.concatenate(
        [first * cosine - second * sine, second * cosine + first * sine], axis=-1
    )


def local(tokens, norm_gain, wq, wk, wv, wo, doc_ids):
    tok_rows = tokens.shape[0]
    head_size = HEAD_WIDTH
    kv_local = wk.shape[1] // head_size
    query_group = QUERY_HEADS // KV_HEAD_COUNT
    source = tokens.astype(jnp.float32)
    whole = lax.all_gather(tokens, "head", axis=1, tiled=True).astype(jnp.float32)
    mean_sq = jnp.mean(whole * whole, axis=1, keepdims=True)
    normed_input = (whole * lax.rsqrt(mean_sq + 1e-05) * norm_gain[None, :]).astype(jnp.bfloat16)
    query_acc = jnp.dot(
        normed_input,
        lax.all_gather(wq, ("seq", "srv"), axis=0, tiled=True),
        preferred_element_type=jnp.float32,
    )
    key_acc = jnp.dot(
        normed_input,
        lax.all_gather(wk, ("seq", "srv"), axis=0, tiled=True),
        preferred_element_type=jnp.float32,
    )
    value_acc = jnp.dot(
        normed_input,
        lax.all_gather(wv, ("seq", "srv"), axis=0, tiled=True),
        preferred_element_type=jnp.float32,
    )
    first_pos = lax.axis_index(("seq", "srv")) * tok_rows
    positions = first_pos + jnp.arange(tok_rows, dtype=jnp.int32)
    query_matrix = rope(query_acc.reshape(tok_rows, kv_local * query_group, head_size), positions)
    query_matrix = query_matrix.astype(jnp.bfloat16).reshape(
        tok_rows, kv_local, query_group, head_size
    )
    key_matrix = rope(key_acc.reshape(tok_rows, kv_local, head_size), positions).astype(
        jnp.bfloat16
    )
    key_matrix = key_matrix.reshape(tok_rows, kv_local * head_size)
    value_matrix = value_acc.astype(jnp.bfloat16)
    scale = 1.0 / head_size**0.5

    def attend_block(carry, key_rows, value_rows, doc_rows, key_pos):
        run_top, run_total, run_acc = carry
        key_heads = key_rows.reshape(key_rows.shape[0], kv_local, head_size)
        value_heads = value_rows.reshape(value_rows.shape[0], kv_local, head_size)
        scores = (
            jnp.einsum(
                "qcgd,kcd->qcgk", query_matrix, key_heads, preferred_element_type=jnp.float32
            )
            * scale
        )
        allowed = (
            (key_pos[None, :] <= positions[:, None])
            & (key_pos[None, :] >= 0)
            & (doc_rows[None, :] == doc_ids[:, None])
        )
        allowed = allowed[:, None, None, :]
        masked = jnp.where(allowed, scores, -1e30)
        new_top = jnp.maximum(run_top, jnp.max(masked, axis=3))
        expd = jnp.where(allowed, jnp.exp(masked - new_top[..., None]), 0.0)
        factor = jnp.exp(run_top - new_top)
        new_total = run_total * factor + jnp.sum(expd, axis=3)
        weights = expd.astype(jnp.bfloat16)
        update = jnp.einsum(
            "qcgk,kcd->qcgd", weights, value_heads, preferred_element_type=jnp.float32
        )
        return (new_top, new_total, run_acc * factor[..., None] + update)

    start_state = (
        jnp.full((tok_rows, kv_local, query_group), -1e30, jnp.float32),
        jnp.zeros((tok_rows, kv_local, query_group), jnp.float32),
        jnp.zeros((tok_rows, kv_local, query_group, head_size), jnp.float32),
    )
    key_piece = lax.all_gather(key_matrix, ("seq", "srv"), axis=0, tiled=True)
    value_piece = lax.all_gather(value_matrix, ("seq", "srv"), axis=0, tiled=True)
    doc_piece = lax.all_gather(doc_ids, ("seq", "srv"), axis=0, tiled=True)
    count = key_piece.shape[0]
    width = math.gcd(count, 512)

    def step(inner, index):
        offset = index * width
        key_rows = lax.dynamic_slice_in_dim(key_piece, offset, width, 0)
        value_rows = lax.dynamic_slice_in_dim(value_piece, offset, width, 0)
        doc_rows = lax.dynamic_slice_in_dim(doc_piece, offset, width, 0)
        key_pos = offset + jnp.arange(width, dtype=jnp.int32)
        return (attend_block(inner, key_rows, value_rows, doc_rows, key_pos), None)

    def run_all(inner):
        result, _ = lax.scan(step, inner, jnp.arange(count // width, dtype=jnp.int32))
        return result

    beyond = jnp.int32(0) > first_pos + tok_rows - 1
    before = doc_piece[count - 1] < doc_ids[0]
    _, final_total, final_acc = lax.cond(beyond | before, lambda inner: inner, run_all, start_state)
    attended = (final_acc / final_total[..., None]).astype(jnp.bfloat16)
    attended = attended.reshape(tok_rows, kv_local * query_group * head_size)
    terms = jnp.dot(
        attended,
        lax.all_gather(wo, ("seq", "srv"), axis=1, tiled=True),
        preferred_element_type=jnp.float32,
    )
    summed = lax.psum_scatter(
        terms.astype(jnp.bfloat16), "head", scatter_dimension=1, tiled=True
    ).astype(jnp.float32)
    return (source + summed).astype(jnp.bfloat16)


def solution(mesh):
    sizes = dict(mesh.shape)
    if sizes["grp"] == 1 and sizes["head"] == 1 and sizes["seq"] == 16 and sizes["srv"] == 2:
        fine = Mesh(np.asarray(mesh.devices).reshape(2, 2, 2, 2, 2), AXES)
        in_specs = (P(AXES), P(), P(AXES), P(AXES), P(AXES), P(None, AXES), P(AXES))
        return jax.shard_map(
            split_body, mesh=fine, in_specs=in_specs, out_specs=P(AXES), check_vma=False
        )
    in_specs = (
        P(("grp", "seq", "srv"), "head"),
        P(),
        P(("seq", "srv"), "head"),
        P(("seq", "srv"), "head"),
        P(("seq", "srv"), "head"),
        P("head", ("seq", "srv")),
        P(("grp", "seq", "srv")),
    )
    out_specs = P(("grp", "seq", "srv"), "head")
    return jax.shard_map(local, mesh=mesh, in_specs=in_specs, out_specs=out_specs, check_vma=False)
```
